128 devices in a mesh: az: 32 (over z, y_lo, x), rad: 4 (over y_hi, core).
Axes of the slice: x: 4, y: 4 (y_hi: 2, y_lo: 2; y = y_hi * 2 + y_lo), z: 4, core: 2. Of those that a mesh axis runs over, the one named last changes fastest.
Arguments:
- state: bfloat16 [4, 64, 2048, 512], P(None, None, 'az', 'rad'), may hold values from -6 to 6
- source: bfloat16 [64, 2048, 512], P(None, 'az', 'rad'), may hold values from -6 to 6
- shear: bfloat16 [64, 2048, 512], P(None, 'az', 'rad'), may hold values from 0.5 to 4
- permeability: bfloat16 [64, 2048, 512], P(None, 'az', 'rad'), may hold values from 0.099609375 to 10
- radial_basis: float32 [512, 512], P('rad'), may hold values from -1 to 2
- radial_eigen: float32 [512], replicated, may hold values from 4e-05 to 4
Outputs:
- correction: bfloat16 [4, 64, 2048, 512], P(None, None, 'az', 'rad')
The draws below stay inside these ranges and needn't reach their ends.
All inputs are finite; a program needn't handle non-finite values.
Results may differ from the reference program's by a relative error of at most 0.001.
Values may be sent and summed in bfloat16 or wider, within the bound.
A program may use at most 192 MiB of HBM per device.

```python
import math
import jax
import jax.numpy as jnp
from jax import lax

NH = 64
NA = 2048
NR = 512


def draw_state(key, part):
    azimuth = jnp.arange(NA, dtype=jnp.float32) / NA
    radius = jnp.arange(NR, dtype=jnp.float32) / NR
    jitter = jax.random.truncated_normal(key, -4.0, 4.0, (4, NH, NA, NR), jnp.float32)
    weight = 0.05 * (10.0 ** azimuth)[:, None] * (3.0 ** radius)[None, :]
    values = weight * jitter
    return values.astype(jnp.bfloat16)


def draw_radial_basis(key, part):
    identity = jnp.eye(NR, dtype=jnp.float32)
    jitter = jax.random.truncated_normal(key, -4.0, 4.0, (NR, NR), jnp.float32) * (0.3 / math.sqrt(NR))
    return identity + jitter


def block_scale(rng, shape, cuts, low, top_value):
    factor_of, own = 1.0, jax.random.fold_in(rng, 6)
    for dim, blocks in cuts:
        steps = jnp.exp(jax.random.uniform(jax.random.fold_in(own, dim), (blocks,), jnp.float32, low / len(cuts), top_value / len(cuts)))
        factor_of = factor_of * jnp.repeat(steps, shape[dim] // blocks).reshape([-1 if axis == dim else 1 for axis in range(len(shape))])
    return factor_of


def noise(key, shape, scale, most, shards=(), kind=jnp.bfloat16):
    values = scale * jax.random.normal(key, shape, jnp.float32)
    if shards:
        values = values * block_scale(key, shape, shards, -0.22, 0.18)
    return jnp.clip(values, -most, most).astype(kind)


def setup_inputs(seed: int = 0) -> dict:
    keys = jax.random.split(jax.random.key(seed), 7)
    return {
        "state": draw_state(jax.random.fold_in(keys[6], 71), 0),
        "source": noise(keys[1], (NH, NA, NR), 1.0, 6.0, ((1, 32), (2, 4))),
        "shear": jnp.clip(jnp.exp(math.log(4.0) - 2.0794415 * jax.random.uniform(keys[2], (NH, NA, NR), jnp.float32) ** block_scale(keys[2], (NH, NA, NR), ((1, 32), (2, 4)), -0.2, 0.2)), 0.5, 4.0).astype(jnp.bfloat16),
        "permeability": jnp.clip(jnp.exp(math.log(10.0) - 4.609084 * jax.random.uniform(keys[3], (NH, NA, NR), jnp.float32) ** block_scale(keys[3], (NH, NA, NR), ((1, 32), (2, 4)), -0.2, 0.2)), 0.099609375, 10.0).astype(jnp.bfloat16),
        "radial_basis": draw_radial_basis(jax.random.fold_in(keys[6], 71), 0),
        "radial_eigen": jnp.clip(jnp.exp(jax.random.uniform(keys[5], (NR,), jnp.float32, math.log(3.9999998989515007e-05), math.log(4.0))), 3.9999998989515007e-05, 4.0),
    }


biot_coupling = 2.0
storage = 1.0

def neighbor(extended, grid_axis, offset):
    lead = extended.ndim - 3
    window = [slice(None)] * lead + [slice(1, -1)] * 3
    length = extended.shape[lead + grid_axis]
    window[lead + grid_axis] = slice(1 + offset, length - 1 + offset)
    return extended[tuple(window)]

def stencil(extended, source_block):
    center = neighbor(extended, 0, 0)
    diagonal = jnp.zeros_like(center[4])
    momentum = [jnp.zeros_like(center[0]), jnp.zeros_like(center[0]), jnp.zeros_like(center[0])]
    fluid = jnp.zeros_like(center[0])
    for grid_axis in (0, 1, 2):
        for offset in (1, -1):
            beside = neighbor(extended, grid_axis, offset)
            shear_face = 0.5 * (center[4] + beside[4])
            flow_face = 0.5 * (center[5] + beside[5])
            diagonal = diagonal + shear_face
            momentum = [momentum[channel] + shear_face * (center[channel] - beside[channel]) for channel in range(3)]
            fluid = fluid + flow_face * (center[3] - beside[3])
    component_axes = (2, 1, 0)
    pressure = extended[3]
    spread = jnp.zeros_like(center[0])
    parts = []
    for channel in range(3):
        grid_axis = component_axes[channel]
        gradient = 0.5 * (neighbor(pressure, grid_axis, 1) - neighbor(pressure, grid_axis, -1))
        parts.append(-(momentum[channel] + biot_coupling * gradient))
        member = extended[channel]
        spread = spread + 0.5 * (neighbor(member, grid_axis, 1) - neighbor(member, grid_axis, -1))
    parts.append(source_block + biot_coupling * spread + storage * center[3] + fluid)
    return (jnp.stack(parts), diagonal)

def cosine_table(extent):
    row_ids = jnp.arange(extent, dtype=jnp.float32)[:, None]
    col_ids = jnp.arange(extent, dtype=jnp.float32)[None, :]
    scaled = jnp.where(row_ids == 0, math.sqrt(1.0 / extent), math.sqrt(2.0 / extent))
    return scaled * jnp.cos(math.pi * (col_ids + 0.5) * row_ids / extent)

def precondition(residual_p, radial_basis, radial_eigen):
    highest = lax.Precision.HIGHEST
    cosine = cosine_table(NH)
    heights = jnp.einsum('lh,har->lar', cosine, residual_p, precision=highest, preferred_element_type=jnp.float32)
    levels = jnp.arange(NH, dtype=jnp.float32)
    height_eigen = 4.0 * jnp.sin(math.pi * levels / (2.0 * NH)) ** 2
    waves = jnp.arange(NA, dtype=jnp.float32)
    azimuth_eigen = 4.0 * jnp.sin(math.pi * waves / NA) ** 2

    def mode_block(inputs):
        plane, level_eigen = inputs
        coeffs = jnp.dot(plane, radial_basis, precision=highest, preferred_element_type=jnp.float32)
        spectral = jnp.fft.fft(coeffs, axis=0)
        totals = storage + radial_eigen[None, :] + level_eigen + azimuth_eigen[:, None]
        solved = jnp.real(jnp.fft.ifft(spectral / totals, axis=0))
        return jnp.dot(solved, radial_basis.T, precision=highest, preferred_element_type=jnp.float32)
    planes = lax.map(mode_block, (heights, height_eigen))
    return jnp.einsum('lh,lar->har', cosine, planes, precision=highest, preferred_element_type=jnp.float32)

def reference(state, source, shear, permeability, radial_basis, radial_eigen):
    layers = jnp.concatenate([state, shear[None], permeability[None]], axis=0)
    layers = jnp.pad(layers, ((0, 0), (1, 1), (0, 0), (1, 1)))
    layers = jnp.concatenate([layers[:, :, -1:], layers, layers[:, :, :1]], axis=2)
    slab_rows = math.gcd(NH, 8)

    def slab(block_index):
        first_row = block_index * slab_rows
        window_part = lax.dynamic_slice_in_dim(layers, first_row, slab_rows + 2, 1).astype(jnp.float32)
        source_part = lax.dynamic_slice_in_dim(source, first_row, slab_rows, 0).astype(jnp.float32)
        residual, diagonal = stencil(window_part, source_part)
        moment_step = residual[:3] / diagonal
        return (moment_step, residual[3], jnp.sum(residual[:3] * residual[:3]), jnp.sum(residual[:3] * moment_step))
    steps, fluid_rows, square_parts, cross_parts = lax.map(slab, jnp.arange(NH // slab_rows, dtype=jnp.int32))
    moment_step = jnp.moveaxis(steps, 0, 1).reshape(3, NH, NA, NR)
    residual_p = fluid_rows.reshape(NH, NA, NR)
    press_step = precondition(residual_p, radial_basis, radial_eigen)
    total_rr = jnp.sum(square_parts) + jnp.sum(residual_p * residual_p)
    total_rz = jnp.sum(cross_parts) + jnp.sum(residual_p * press_step)
    alpha = total_rr / total_rz
    return jnp.concatenate([(alpha * moment_step).astype(jnp.bfloat16), (alpha * press_step).astype(jnp.bfloat16)[None]], axis=0)
```

```python
import functools
import math

import jax
import jax.numpy as jnp
import numpy as np
from jax import lax
from jax.experimental import pallas as pl
from jax.experimental.pallas import tpu as pltpu
from jax.sharding import PartitionSpec as P

NH = 64
BA = 64
BR = 128
NRAD = 4
NAZ = 32
LV = NH // NRAD
NM = NRAD * BR
CA = 8
NCH = BA // CA
HB = 4
ROW = 80
PAD = 8

BIOT = 2.0
STORAGE = 1.0

F32 = jnp.float32
BF16 = jnp.bfloat16
WIRE = F32
MESH = pl.DeviceIdType.MESH

ORDER = (3, 5, 0, 1, 2, 4)


def split(x):
    hi = x.astype(BF16)
    lo = (x - hi.astype(F32)).astype(BF16)
    return hi, lo


def cosine_tables():
    l = np.arange(NH, dtype=np.float64)[:, None]
    h = np.arange(NH, dtype=np.float64)[None, :]
    scale = np.where(l == 0, math.sqrt(1.0 / NH), math.sqrt(2.0 / NH))
    table = jnp.asarray(scale * np.cos(math.pi * (h + 0.5) * l / NH), F32)
    out = []
    for c in (table, table.T):
        hi, lo = split(c)
        out.append(jnp.concatenate([hi, lo, hi], axis=1))
    return out


def remote(src, dst, send, recv, device):
    return pltpu.make_async_remote_copy(
        src_ref=src, dst_ref=dst, send_sem=send, recv_sem=recv,
        device_id=device, device_id_type=MESH,
    )


def dot(a, b, dims=((1,), (0,))):
    return lax.dot_general(a, b, (dims, ((), ())), preferred_element_type=F32)


def dot3(xh, xl, bh, bl, dims):
    return dot(xh, bh, dims) + (dot(xl, bh, dims) + dot(xh, bl, dims))


def kernel(
    state, source, shear, perm, basis, eigen, fwd_tab, inv_tab, out,
    xb, ext, qs, ql, qr, pk, ahs, ahr, ah32,
    tmp, mom, fs, fr, coef, ysol, gq, gs, gr, pr,
    bas, bhi, blo, cs, cr, acc, red, redr,
    in_sem, out_sem, hs, hr, as_, ar_, bs, br_, fss, frs, gss, grs, css, crs, rss, rrs,
):
    az = lax.axis_index("az")
    rad = lax.axis_index("rad")
    mate = rad + 1 - 2 * lax.rem(rad, 2)
    across = lax.rem(rad + 2, NRAD)
    az_up = lax.rem(az + 1, NAZ)
    az_dn = lax.rem(az + NAZ - 1, NAZ)
    rad_up = lax.rem(rad + 1, NRAD)
    rad_dn = lax.rem(rad + NRAD - 1, NRAD)
    axx = lax.rem(az, 4)
    azy = az // 4
    x_peers = [(azy * 4 + lax.rem(axx + d, 4), rad) for d in range(1, 4)]
    zy_peers = [(lax.rem(azy + d, 8) * 4 + axx, rad) for d in range(1, 8)]
    rad_peers = [(az, lax.rem(rad + d, NRAD)) for d in range(1, NRAD)]

    def load(f):
        if f < 4:
            src = state.at[f]
        else:
            src = (shear, perm)[f - 4]
        return pltpu.make_async_copy(src, xb.at[f], in_sem.at[f])

    for f in ORDER:
        load(f).start()
    own_basis = pltpu.make_async_copy(basis, bas.at[rad], in_sem.at[7])
    own_basis.start()
    src_load = pltpu.make_async_copy(source, xb.at[6], in_sem.at[6])
    src_load.start()

    barrier = pltpu.get_barrier_semaphore()
    partners = rad_peers + x_peers + zy_peers + [(az_up, rad), (az_dn, rad)]
    for peer in partners:
        pl.semaphore_signal(barrier, inc=1, device_id=peer, device_id_type=MESH)
    pl.semaphore_wait(barrier, len(partners))

    lane = lax.broadcasted_iota(jnp.int32, (BA, BR), 1)
    zero_row = jnp.zeros((ROW, BR), F32)
    halo = []
    for n, f in enumerate(ORDER):
        load(f).wait()
        ext[f, 0] = zero_row
        ext[f, NH + 1] = zero_row

        def stage(h, q, f=f):
            x = xb[f, h].astype(F32)
            ext[f, h + 1, pl.ds(PAD, BA), :] = x
            ah32[0, pl.ds(h, 1), :] = x[0:1]
            ah32[1, pl.ds(h, 1), :] = x[BA - 1 : BA]
            rolled = pltpu.roll(x, 2 * h + 1, 1)
            return jnp.where(lane // 2 == h, rolled, q)

        q = lax.fori_loop(0, NH, stage, jnp.zeros((BA, BR), F32))
        qs[f] = q.astype(BF16)
        ahs[f, 0] = ah32[0].astype(BF16)
        ahs[f, 1] = ah32[1].astype(BF16)
        one = [
            remote(qs.at[f], ql.at[f], hs.at[f, 0], hr.at[f, 0], (az, rad_up)),
            remote(qs.at[f], qr.at[f], hs.at[f, 1], hr.at[f, 1], (az, rad_dn)),
            remote(ahs.at[f, 1], ahr.at[f, 0], as_.at[f, 0], ar_.at[f, 0], (az_up, rad)),
            remote(ahs.at[f, 0], ahr.at[f, 1], as_.at[f, 1], ar_.at[f, 1], (az_dn, rad)),
        ]
        for c in one:
            c.start()
        halo.append((f, one))

    own_basis.wait()
    b_mate = remote(bas.at[rad], bas.at[rad], bs.at[0], br_.at[0], (az, mate))
    b_across = remote(bas.at[rad], bas.at[rad], bs.at[1], br_.at[1], (az, across))
    b_relay = remote(bas.at[across], bas.at[across], bs.at[2], br_.at[2], (az, mate))
    b_mate.start()
    b_across.start()

    even = lax.rem(lane, 2) == 0

    def finish_halo(entry):
        f, one = entry
        for c in one:
            c.wait_recv()
        left = jnp.where(rad > 0, ql[f].astype(F32), 0.0)
        right = jnp.where(rad < NRAD - 1, qr[f].astype(F32), 0.0)
        pk[f] = jnp.where(even, pltpu.roll(right, BR - 1, 1), pltpu.roll(left, 1, 1))
        ah32[0] = ahr[f, 0].astype(F32)
        ah32[1] = ahr[f, 1].astype(F32)

        def place(h, carry):
            ext[f, h + 1, pl.ds(PAD - 1, 1), :] = ah32[0, pl.ds(h, 1), :]
            ext[f, h + 1, pl.ds(PAD + BA, 1), :] = ah32[1, pl.ds(h, 1), :]
            return carry

        lax.fori_loop(0, NH, place, 0)

    for entry in halo[:5]:
        finish_halo(entry)

    lane3 = lax.broadcasted_iota(jnp.int32, (HB, CA, BR), 2)
    first = lane3 == 0
    last = lane3 == BR - 1

    def block(f, h0, c, dh=0, da=0):
        return ext[f, pl.ds(h0 + 1 + dh, HB), pl.ds(PAD + CA * c + da, CA), :]

    def radial_pair(f, h0, c, v):
        tile = pk[f, pl.ds(pl.multiple_of(CA * c, CA), CA), :]
        ends = jnp.stack([pltpu.roll(tile, 127 - 2 * (h0 + i), 1) for i in range(HB)])
        up = jnp.where(last, ends, pltpu.roll(v, BR - 1, 2))
        down = jnp.where(first, ends, pltpu.roll(v, 1, 2))
        return up, down

    def neighbours(f, h0, c):
        v = block(f, h0, c)
        up, down = radial_pair(f, h0, c, v)
        return v, (
            (block(f, h0, c, dh=1), block(f, h0, c, dh=-1)),
            (block(f, h0, c, da=1), block(f, h0, c, da=-1)),
            (up, down),
        )

    src_load.wait()

    def fluid_chunk(c, rr):
        def rows(b, rr):
            h0 = b * HB
            k, ks = neighbours(5, h0, c)
            p, ps = neighbours(3, h0, c)
            total = jnp.zeros_like(p)
            for axis in range(3):
                for side in range(2):
                    total = total + (k + ks[axis][side]) * (p - ps[axis][side])
            u0 = block(0, h0, c)
            up, down = radial_pair(0, h0, c, u0)
            spread = up - down
            spread = spread + (block(1, h0, c, da=1) - block(1, h0, c, da=-1))
            spread = spread + (block(2, h0, c, dh=1) - block(2, h0, c, dh=-1))
            s = xb[6, pl.ds(h0, HB), pl.ds(pl.multiple_of(2 * CA * (c // 2), 2 * CA), 2 * CA), :].astype(F32)
            s = jnp.where(lax.rem(c, 2) == 0, s[:, :CA], s[:, CA:])
            res = s + (0.5 * BIOT) * spread + STORAGE * p + 0.5 * total
            tmp[pl.ds(pl.multiple_of(h0 * CA, CA), HB * CA), :] = res.reshape(HB * CA, BR)
            return rr + jnp.sum(res * res, axis=0)

        rr = lax.fori_loop(0, NH // HB, rows, rr)
        table = fwd_tab[...]
        for pair in range(CA // 2):
            cols = []
            for i in range(2):
                x = tmp[pl.ds(2 * pair + i, NH, stride=CA), :]
                hi, lo = split(x)
                cols.append(jnp.concatenate([hi, hi, lo], axis=0))
            y = dot(table, jnp.concatenate(cols, axis=1))
            for i in range(2):
                for d in range(NRAD):
                    fs[d, c * CA + 2 * pair + i] = y[LV * d : LV * (d + 1), BR * i : BR * (i + 1)].astype(WIRE)
        for d in range(1, NRAD):
            fwd_copy(c, d).start()
        return rr

    def fwd_copy(c, d):
        t = lax.rem(rad + d, NRAD)
        sl = pl.ds(c * CA, CA)
        return remote(fs.at[t, sl], fr.at[rad, sl], fss.at[d, c], frs.at[d, c], (az, t))

    rr = lax.fori_loop(0, NCH, fluid_chunk, jnp.zeros((CA, BR), F32))

    b_across.wait_recv()
    b_relay.start()
    finish_halo(halo[5])

    def moment_chunk(c, carry):
        def rows(b, carry):
            rr, rz = carry
            h0 = b * HB
            g, gs_ = neighbours(4, h0, c)
            face = [[g + gs_[axis][side] for side in range(2)] for axis in range(3)]
            diag2 = (face[0][0] + face[0][1]) + (face[1][0] + face[1][1]) + (face[2][0] + face[2][1])
            p = block(3, h0, c)
            up, down = radial_pair(3, h0, c, p)
            grads = (
                up - down,
                block(3, h0, c, da=1) - block(3, h0, c, da=-1),
                block(3, h0, c, dh=1) - block(3, h0, c, dh=-1),
            )
            inv = 2.0 / diag2
            for f in range(3):
                u, us = neighbours(f, h0, c)
                total = jnp.zeros_like(u)
                for axis in range(3):
                    for side in range(2):
                        total = total + face[axis][side] * (u - us[axis][side])
                res = -(0.5 * total + (0.5 * BIOT) * grads[f])
                step = res * inv
                mom[f, pl.ds(h0, HB), pl.ds(pl.multiple_of(CA * c, CA), CA), :] = step
                rr = rr + jnp.sum(res * res, axis=0)
                rz = rz + jnp.sum(res * step, axis=0)
            return rr, rz

        return lax.fori_loop(0, NH // HB, rows, carry)

    rr, rz = lax.fori_loop(0, NCH, moment_chunk, (rr, jnp.zeros((CA, BR), F32)))
    acc[pl.ds(0, CA), :] = rr

    b_mate.wait_recv()
    b_relay.wait_recv()
    for j in range(NRAD):
        hi, lo = split(bas[j])
        bhi[pl.ds(j * BR, BR), :] = hi
        blo[pl.ds(j * BR, BR), :] = lo

    level = (lax.broadcasted_iota(jnp.int32, (LV, NM), 0) + LV * rad).astype(F32)
    half = jnp.sin(level * (math.pi / (2.0 * NH)))
    sigma = STORAGE + eigen[...] + 4.0 * half * half
    root = jnp.sqrt(sigma * (sigma + 4.0))
    lam = 2.0 / (sigma + 2.0 + root)
    inv_root = 1.0 / root

    def fwd_chunk(c, carry):
        y, w, power = carry
        for d in range(1, NRAD):
            src = lax.rem(rad + NRAD - d, NRAD)
            sl = pl.ds(c * CA, CA)
            remote(fs.at[src, sl], fr.at[src, sl], fss.at[d, c], frs.at[d, c], (az, src)).wait_recv()
        fr[rad, pl.ds(c * CA, CA)] = fs[rad, pl.ds(c * CA, CA)]
        x = jnp.concatenate(
            [fr[j, pl.ds(c * CA, CA)].astype(F32).reshape(CA * LV, BR) for j in range(NRAD)], axis=1
        )
        hi, lo = split(x)
        z = dot3(hi, lo, bhi[...], blo[...], ((1,), (0,)))
        coef[pl.ds(pl.multiple_of(c * CA * LV, CA * LV), CA * LV), :] = z
        for i in range(CA):
            f = z[i * LV : (i + 1) * LV]
            y = lam * y + f
            w = w + power * f
            power = power * lam
        return y, w, power

    zero = jnp.zeros((LV, NM), F32)
    y, w, _ = lax.fori_loop(0, NCH, fwd_chunk, (zero, zero, jnp.ones((LV, NM), F32)))
    cs[0] = y
    cs[1] = w
    c_up = remote(cs.at[0], cr.at[0], css.at[0], crs.at[0], (az_up, rad))
    c_dn = remote(cs.at[1], cr.at[1], css.at[1], crs.at[1], (az_dn, rad))
    c_up.start()
    c_dn.start()
    c_up.wait_recv()

    def sweep_up(a, y):
        rows = pl.ds(pl.multiple_of(a * LV, LV), LV)
        y = lam * y + coef[rows, :]
        ysol[rows, :] = y
        return y

    lax.fori_loop(0, BA, sweep_up, cr[0])
    c_dn.wait_recv()

    def back_copy(c, d):
        t = lax.rem(rad + d, NRAD)
        sl = pl.ds(c * CA, CA)
        return remote(gs.at[t, sl], gr.at[rad, sl], gss.at[d, c], grs.at[d, c], (az, t))

    def back_chunk(n, carry):
        w, fq = carry
        c = NCH - 1 - n

        def cell(i, carry):
            w, fq = carry
            a = CA - 1 - i
            rows = pl.ds(pl.multiple_of((c * CA + a) * LV, LV), LV)
            f = coef[rows, :]
            lw = lam * w
            q = (ysol[rows, :] + lw) * inv_root
            gq[pl.ds(pl.multiple_of(a * LV, LV), LV), :] = q
            return f + lw, fq + f * q

        w, fq = lax.fori_loop(0, CA, cell, (w, fq))
        hi, lo = split(gq[...])
        z = dot3(hi, lo, bhi[...], blo[...], ((1,), (1,)))
        for j in range(NRAD):
            gs[j, pl.ds(c * CA, CA)] = z[:, BR * j : BR * (j + 1)].reshape(CA, LV, BR).astype(WIRE)
        for d in range(1, NRAD):
            back_copy(c, d).start()
        return w, fq

    _, fq = lax.fori_loop(0, NCH, back_chunk, (cr[1], zero))
    part = rz
    for i in range(LV // CA):
        for j in range(NRAD):
            part = part + fq[CA * i : CA * (i + 1), BR * j : BR * (j + 1)]
    acc[pl.ds(CA, CA), :] = part

    total = acc[...]
    base = 0
    for slot, group in enumerate((rad_peers, x_peers, zy_peers)):
        red[slot] = total
        copies = [
            remote(red.at[slot], redr.at[base + i], rss.at[base + i], rrs.at[base + i], peer)
            for i, peer in enumerate(group)
        ]
        for c in copies:
            c.start()
        for i, c in enumerate(copies):
            c.wait_recv()
            total = total + redr[base + i]
        base += len(group)
    alpha = jnp.sum(total[:CA]) / jnp.sum(total[CA:])

    def scale_row(h, carry):
        for f in range(3):
            xb[f, h] = (alpha * mom[f, h]).astype(BF16)
        return carry

    lax.fori_loop(0, NH, scale_row, 0)
    outs = [pltpu.make_async_copy(xb.at[f], out.at[f], out_sem.at[f]) for f in range(3)]
    for o in outs:
        o.start()

    def last_chunk(n, carry):
        c = BA // 16 - 1 - n
        for half_ in range(2):
            cc = 2 * c + 1 - half_
            for d in range(1, NRAD):
                src = lax.rem(rad + NRAD - d, NRAD)
                sl = pl.ds(cc * CA, CA)
                remote(gs.at[src, sl], gr.at[src, sl], gss.at[d, cc], grs.at[d, cc], (az, src)).wait_recv()
        gr[rad, pl.ds(c * 16, 16)] = gs[rad, pl.ds(c * 16, 16)]
        table = inv_tab[...]
        for pair in range(8):
            cols = []
            for i in range(2):
                a = c * 16 + 2 * pair + i
                x = jnp.concatenate([gr[j, a].astype(F32) for j in range(NRAD)], axis=0)
                hi, lo = split(x)
                cols.append(jnp.concatenate([hi, hi, lo], axis=0))
            y = dot(table, jnp.concatenate(cols, axis=1)) * alpha
            for i in range(2):
                pr[pl.ds(2 * pair + i, NH, stride=16), :] = y[:, BR * i : BR * (i + 1)]

        def rows(h, carry):
            xb[3, h, pl.ds(pl.multiple_of(c * 16, 16), 16), :] = pr[pl.ds(pl.multiple_of(h * 16, 16), 16), :].astype(BF16)
            return carry

        lax.fori_loop(0, NH, rows, 0)
        sl = pl.ds(pl.multiple_of(c * 16, 16), 16)
        pltpu.make_async_copy(xb.at[3, :, sl], out.at[3, :, sl], out_sem.at[3 + c]).start()
        return carry

    lax.fori_loop(0, BA // 16, last_chunk, 0)

    for o in outs:
        o.wait()
    for c in range(BA // 16):
        sl = pl.ds(c * 16, 16)
        pltpu.make_async_copy(xb.at[3, :, sl], out.at[3, :, sl], out_sem.at[3 + c]).wait()
    for f, one in halo:
        for c in one:
            c.wait_send()
    for c in (b_mate, b_across, b_relay, c_up, c_dn):
        c.wait_send()
    base = 0
    for slot, group in enumerate((rad_peers, x_peers, zy_peers)):
        for i, peer in enumerate(group):
            remote(red.at[slot], redr.at[base + i], rss.at[base + i], rrs.at[base + i], peer).wait_send()
        base += len(group)

    def drain(c, carry):
        for d in range(1, NRAD):
            fwd_copy(c, d).wait_send()
            back_copy(c, d).wait_send()
        return carry

    lax.fori_loop(0, NCH, drain, 0)


def body(state, source, shear, permeability, radial_basis, radial_eigen):
    fwd_tab, inv_tab = cosine_tables()
    anyspace = pl.BlockSpec(memory_space=pl.ANY)
    vmem = pl.BlockSpec(memory_space=pltpu.VMEM)
    dma = pltpu.SemaphoreType.DMA
    scratch = [
        pltpu.VMEM((7, NH, BA, BR), BF16),
        pltpu.VMEM((6, NH + 2, ROW, BR), F32),
        pltpu.VMEM((6, BA, BR), BF16),
        pltpu.VMEM((6, BA, BR), BF16),
        pltpu.VMEM((6, BA, BR), BF16),
        pltpu.VMEM((6, BA, BR), F32),
        pltpu.VMEM((6, 2, NH, BR), BF16),
        pltpu.VMEM((6, 2, NH, BR), BF16),
        pltpu.VMEM((2, NH, BR), F32),
        pltpu.VMEM((NH * CA, BR), F32),
        pltpu.VMEM((3, NH, BA, BR), F32),
        pltpu.VMEM((NRAD, BA, LV, BR), WIRE),
        pltpu.VMEM((NRAD, BA, LV, BR), WIRE),
        pltpu.VMEM((BA * LV, NM), F32),
        pltpu.VMEM((BA * LV, NM), F32),
        pltpu.VMEM((CA * LV, NM), F32),
        pltpu.VMEM((NRAD, BA, LV, BR), WIRE),
        pltpu.VMEM((NRAD, BA, LV, BR), WIRE),
        pltpu.VMEM((NH * 16, BR), F32),
        pltpu.VMEM((NRAD, BR, NM), F32),
        pltpu.VMEM((NM, NM), BF16),
        pltpu.VMEM((NM, NM), BF16),
        pltpu.VMEM((2, LV, NM), F32),
        pltpu.VMEM((2, LV, NM), F32),
        pltpu.VMEM((2 * CA, BR), F32),
        pltpu.VMEM((3, 2 * CA, BR), F32),
        pltpu.VMEM((13, 2 * CA, BR), F32),
        dma((8,)), dma((8,)),
        dma((6, 2)), dma((6, 2)), dma((6, 2)), dma((6, 2)),
        dma((3,)), dma((3,)),
        dma((NRAD, NCH)), dma((NRAD, NCH)), dma((NRAD, NCH)), dma((NRAD, NCH)),
        dma((2,)), dma((2,)),
        dma((13,)), dma((13,)),
    ]
    return pl.pallas_call(
        kernel,
        out_shape=jax.ShapeDtypeStruct((4, NH, BA, BR), BF16),
        in_specs=[anyspace] * 5 + [vmem] * 3,
        out_specs=anyspace,
        scratch_shapes=scratch,
        compiler_params=pltpu.CompilerParams(
            collective_id=0, has_side_effects=True, vmem_limit_bytes=60 << 20
        ),
        name="residual_step",
    )(state, source, shear, permeability, radial_basis, radial_eigen.reshape(1, NM), fwd_tab, inv_tab)


def solution(mesh):
    placed = (
        P(None, None, "az", "rad"),
        P(None, "az", "rad"),
        P(None, "az", "rad"),
        P(None, "az", "rad"),
        P("rad", None),
        P(),
    )
    return jax.shard_map(
        body, mesh=mesh, in_specs=placed, out_specs=P(None, None, "az", "rad"), check_vma=False
    )
```

```python
import functools
import math

import jax
import jax.numpy as jnp
import numpy as np
from jax import lax
from jax.experimental import pallas as pl
from jax.experimental.pallas import tpu as pltpu
from jax.sharding import PartitionSpec as P

NH = 64
BA = 64
BR = 128
NRAD = 4
NAZ = 32
LV = NH // NRAD
NM = NRAD * BR
CA = 8
NCH = BA // CA
HB = 4
ROW = 80
PAD = 8

BIOT = 2.0
STORAGE = 1.0

F32 = jnp.float32
BF16 = jnp.bfloat16
WIRE = F32
MESH = pl.DeviceIdType.MESH

ORDER = (3, 5, 0, 1, 2, 4)


def split(x):
    hi = x.astype(BF16)
    lo = (x - hi.astype(F32)).astype(BF16)
    return hi, lo


def cosine_tables():
    l = np.arange(NH, dtype=np.float64)[:, None]
    h = np.arange(NH, dtype=np.float64)[None, :]
    scale = np.where(l == 0, math.sqrt(1.0 / NH), math.sqrt(2.0 / NH))
    table = jnp.asarray(scale * np.cos(math.pi * (h + 0.5) * l / NH), F32)
    out = []
    for c in (table, table.T):
        hi, lo = split(c)
        out.append(jnp.concatenate([hi, lo, hi], axis=1))
    return out


def remote(src, dst, send, recv, device):
    return pltpu.make_async_remote_copy(
        src_ref=src, dst_ref=dst, send_sem=send, recv_sem=recv,
        device_id=device, device_id_type=MESH,
    )


def dot(a, b, dims=((1,), (0,))):
    return lax.dot_general(a, b, (dims, ((), ())), preferred_element_type=F32)


def dot3(xh, xl, bh, bl, dims):
    return dot(xh, bh, dims) + (dot(xl, bh, dims) + dot(xh, bl, dims))


def kernel(
    state, source, shear, perm, basis, eigen, fwd_tab, inv_tab, out,
    xb, ext, qs, ql, qr, pk, ahs, ahr, ah32,
    tmp, mom, fs, fr, coef, ysol, gq, gs, gr, pr,
    bas, bhi, blo, cs, cr, acc, red, redr,
    in_sem, out_sem, hs, hr, as_, ar_, bs, br_, fss, frs, gss, grs, css, crs, rss, rrs,
):
    az = lax.axis_index("az")
    rad = lax.axis_index("rad")
    mate = rad + 1 - 2 * lax.rem(rad, 2)
    across = lax.rem(rad + 2, NRAD)
    az_up = lax.rem(az + 1, NAZ)
    az_dn = lax.rem(az + NAZ - 1, NAZ)
    rad_up = lax.rem(rad + 1, NRAD)
    rad_dn = lax.rem(rad + NRAD - 1, NRAD)
    axx = lax.rem(az, 4)
    azy = az // 4
    x_peers = [(azy * 4 + lax.rem(axx + d, 4), rad) for d in range(1, 4)]
    zy_peers = [(lax.rem(azy + d, 8) * 4 + axx, rad) for d in range(1, 8)]
    rad_peers = [(az, lax.rem(rad + d, NRAD)) for d in range(1, NRAD)]

    def load(f):
        if f < 4:
            src = state.at[f]
        else:
            src = (shear, perm)[f - 4]
        return pltpu.make_async_copy(src, xb.at[f], in_sem.at[f])

    for f in ORDER:
        load(f).start()
    own_basis = pltpu.make_async_copy(basis, bas.at[rad], in_sem.at[7])
    own_basis.start()
    src_load = pltpu.make_async_copy(source, xb.at[6], in_sem.at[6])
    src_load.start()

    barrier = pltpu.get_barrier_semaphore()
    partners = rad_peers + x_peers + zy_peers + [(az_up, rad), (az_dn, rad)]
    for peer in partners:
        pl.semaphore_signal(barrier, inc=1, device_id=peer, device_id_type=MESH)
    pl.semaphore_wait(barrier, len(partners))

    lane = lax.broadcasted_iota(jnp.int32, (BA, BR), 1)
    zero_row = jnp.zeros((ROW, BR), F32)
    halo = []
    for n, f in enumerate(ORDER):
        load(f).wait()
        ext[f, 0] = zero_row
        ext[f, NH + 1] = zero_row

        def stage(h, q, f=f):
            x = xb[f, h].astype(F32)
            ext[f, h + 1, pl.ds(PAD, BA), :] = x
            ah32[0, pl.ds(h, 1), :] = x[0:1]
            ah32[1, pl.ds(h, 1), :] = x[BA - 1 : BA]
            rolled = pltpu.roll(x, 2 * h + 1, 1)
            return jnp.where(lane // 2 == h, rolled, q)

        q = lax.fori_loop(0, NH, stage, jnp.zeros((BA, BR), F32), unroll=8)
        qs[f] = q.astype(BF16)
        ahs[f, 0] = ah32[0].astype(BF16)
        ahs[f, 1] = ah32[1].astype(BF16)
        one = [
            remote(qs.at[f], ql.at[f], hs.at[f, 0], hr.at[f, 0], (az, rad_up)),
            remote(qs.at[f], qr.at[f], hs.at[f, 1], hr.at[f, 1], (az, rad_dn)),
            remote(ahs.at[f, 1], ahr.at[f, 0], as_.at[f, 0], ar_.at[f, 0], (az_up, rad)),
            remote(ahs.at[f, 0], ahr.at[f, 1], as_.at[f, 1], ar_.at[f, 1], (az_dn, rad)),
        ]
        for c in one:
            c.start()
        halo.append((f, one))

    own_basis.wait()
    b_mate = remote(bas.at[rad], bas.at[rad], bs.at[0], br_.at[0], (az, mate))
    b_across = remote(bas.at[rad], bas.at[rad], bs.at[1], br_.at[1], (az, across))
    b_relay = remote(bas.at[across], bas.at[across], bs.at[2], br_.at[2], (az, mate))
    b_mate.start()
    b_across.start()

    even = lax.rem(lane, 2) == 0

    def finish_halo(entry):
        f, one = entry
        for c in one:
            c.wait_recv()
        left = jnp.where(rad > 0, ql[f].astype(F32), 0.0)
        right = jnp.where(rad < NRAD - 1, qr[f].astype(F32), 0.0)
        pk[f] = jnp.where(even, pltpu.roll(right, BR - 1, 1), pltpu.roll(left, 1, 1))
        ah32[0] = ahr[f, 0].astype(F32)
        ah32[1] = ahr[f, 1].astype(F32)

        def place(h, carry):
            ext[f, h + 1, pl.ds(PAD - 1, 1), :] = ah32[0, pl.ds(h, 1), :]
            ext[f, h + 1, pl.ds(PAD + BA, 1), :] = ah32[1, pl.ds(h, 1), :]
            return carry

        lax.fori_loop(0, NH, place, 0, unroll=8)

    for entry in halo[:5]:
        finish_halo(entry)

    lane3 = lax.broadcasted_iota(jnp.int32, (HB, CA, BR), 2)
    first = lane3 == 0
    last = lane3 == BR - 1

    def block(f, h0, c, dh=0, da=0):
        return ext[f, pl.ds(h0 + 1 + dh, HB), pl.ds(PAD + CA * c + da, CA), :]

    def radial_pair(f, h0, c, v):
        tile = pk[f, pl.ds(pl.multiple_of(CA * c, CA), CA), :]
        ends = jnp.stack([pltpu.roll(tile, 127 - 2 * (h0 + i), 1) for i in range(HB)])
        up = jnp.where(last, ends, pltpu.roll(v, BR - 1, 2))
        down = jnp.where(first, ends, pltpu.roll(v, 1, 2))
        return up, down

    def neighbours(f, h0, c):
        v = block(f, h0, c)
        up, down = radial_pair(f, h0, c, v)
        return v, (
            (block(f, h0, c, dh=1), block(f, h0, c, dh=-1)),
            (block(f, h0, c, da=1), block(f, h0, c, da=-1)),
            (up, down),
        )

    src_load.wait()

    def fluid_chunk(c, rr):
        def rows(b, rr):
            h0 = b * HB
            k, ks = neighbours(5, h0, c)
            p, ps = neighbours(3, h0, c)
            total = jnp.zeros_like(p)
            for axis in range(3):
                for side in range(2):
                    total = total + (k + ks[axis][side]) * (p - ps[axis][side])
            u0 = block(0, h0, c)
            up, down = radial_pair(0, h0, c, u0)
            spread = up - down
            spread = spread + (block(1, h0, c, da=1) - block(1, h0, c, da=-1))
            spread = spread + (block(2, h0, c, dh=1) - block(2, h0, c, dh=-1))
            s = xb[6, pl.ds(h0, HB), pl.ds(pl.multiple_of(2 * CA * (c // 2), 2 * CA), 2 * CA), :].astype(F32)
            s = jnp.where(lax.rem(c, 2) == 0, s[:, :CA], s[:, CA:])
            res = s + (0.5 * BIOT) * spread + STORAGE * p + 0.5 * total
            tmp[pl.ds(pl.multiple_of(h0 * CA, CA), HB * CA), :] = res.reshape(HB * CA, BR)
            return rr + jnp.sum(res * res, axis=0)

        rr = lax.fori_loop(0, NH // HB, rows, rr, unroll=4)
        table = fwd_tab[...]
        for pair in range(CA // 2):
            cols = []
            for i in range(2):
                x = tmp[pl.ds(2 * pair + i, NH, stride=CA), :]
                hi, lo = split(x)
                cols.append(jnp.concatenate([hi, hi, lo], axis=0))
            y = dot(table, jnp.concatenate(cols, axis=1))
            for i in range(2):
                for d in range(NRAD):
                    fs[d, c * CA + 2 * pair + i] = y[LV * d : LV * (d + 1), BR * i : BR * (i + 1)].astype(WIRE)
        for d in range(1, NRAD):
            fwd_copy(c, d).start()
        return rr

    def fwd_copy(c, d):
        t = lax.rem(rad + d, NRAD)
        sl = pl.ds(c * CA, CA)
        return remote(fs.at[t, sl], fr.at[rad, sl], fss.at[d, c], frs.at[d, c], (az, t))

    rr = lax.fori_loop(0, NCH, fluid_chunk, jnp.zeros((CA, BR), F32))

    b_across.wait_recv()
    b_relay.start()
    finish_halo(halo[5])

    def moment_chunk(c, carry):
        def rows(b, carry):
            rr, rz = carry
            h0 = b * HB
            g, gs_ = neighbours(4, h0, c)
            face = [[g + gs_[axis][side] for side in range(2)] for axis in range(3)]
            diag2 = (face[0][0] + face[0][1]) + (face[1][0] + face[1][1]) + (face[2][0] + face[2][1])
            p = block(3, h0, c)
            up, down = radial_pair(3, h0, c, p)
            grads = (
                up - down,
                block(3, h0, c, da=1) - block(3, h0, c, da=-1),
                block(3, h0, c, dh=1) - block(3, h0, c, dh=-1),
            )
            inv = 2.0 / diag2
            for f in range(3):
                u, us = neighbours(f, h0, c)
                total = jnp.zeros_like(u)
                for axis in range(3):
                    for side in range(2):
                        total = total + face[axis][side] * (u - us[axis][side])
                res = -(0.5 * total + (0.5 * BIOT) * grads[f])
                step = res * inv
                mom[f, pl.ds(h0, HB), pl.ds(pl.multiple_of(CA * c, CA), CA), :] = step
                rr = rr + jnp.sum(res * res, axis=0)
                rz = rz + jnp.sum(res * step, axis=0)
            return rr, rz

        return lax.fori_loop(0, NH // HB, rows, carry, unroll=4)

    rr, rz = lax.fori_loop(0, NCH, moment_chunk, (rr, jnp.zeros((CA, BR), F32)))
    acc[pl.ds(0, CA), :] = rr

    b_mate.wait_recv()
    b_relay.wait_recv()
    for j in range(NRAD):
        hi, lo = split(bas[j])
        bhi[pl.ds(j * BR, BR), :] = hi
        blo[pl.ds(j * BR, BR), :] = lo

    level = (lax.broadcasted_iota(jnp.int32, (LV, NM), 0) + LV * rad).astype(F32)
    half = jnp.sin(level * (math.pi / (2.0 * NH)))
    sigma = STORAGE + eigen[...] + 4.0 * half * half
    root = jnp.sqrt(sigma * (sigma + 4.0))
    lam = 2.0 / (sigma + 2.0 + root)
    inv_root = 1.0 / root

    def fwd_chunk(c, carry):
        y, w, power = carry
        for d in range(1, NRAD):
            src = lax.rem(rad + NRAD - d, NRAD)
            sl = pl.ds(c * CA, CA)
            remote(fs.at[src, sl], fr.at[src, sl], fss.at[d, c], frs.at[d, c], (az, src)).wait_recv()
        fr[rad, pl.ds(c * CA, CA)] = fs[rad, pl.ds(c * CA, CA)]
        x = jnp.concatenate(
            [fr[j, pl.ds(c * CA, CA)].astype(F32).reshape(CA * LV, BR) for j in range(NRAD)], axis=1
        )
        hi, lo = split(x)
        z = dot3(hi, lo, bhi[...], blo[...], ((1,), (0,)))
        coef[pl.ds(pl.multiple_of(c * CA * LV, CA * LV), CA * LV), :] = z
        for i in range(CA):
            f = z[i * LV : (i + 1) * LV]
            y = lam * y + f
            w = w + power * f
            power = power * lam
        return y, w, power

    zero = jnp.zeros((LV, NM), F32)
    y, w, _ = lax.fori_loop(0, NCH, fwd_chunk, (zero, zero, jnp.ones((LV, NM), F32)))
    cs[0] = y
    cs[1] = w
    c_up = remote(cs.at[0], cr.at[0], css.at[0], crs.at[0], (az_up, rad))
    c_dn = remote(cs.at[1], cr.at[1], css.at[1], crs.at[1], (az_dn, rad))
    c_up.start()
    c_dn.start()
    c_up.wait_recv()

    def sweep_up(a, y):
        rows = pl.ds(pl.multiple_of(a * LV, LV), LV)
        y = lam * y + coef[rows, :]
        ysol[rows, :] = y
        return y

    lax.fori_loop(0, BA, sweep_up, cr[0], unroll=8)
    c_dn.wait_recv()

    def back_copy(c, d):
        t = lax.rem(rad + d, NRAD)
        sl = pl.ds(c * CA, CA)
        return remote(gs.at[t, sl], gr.at[rad, sl], gss.at[d, c], grs.at[d, c], (az, t))

    def back_chunk(n, carry):
        w, fq = carry
        c = NCH - 1 - n

        def cell(i, carry):
            w, fq = carry
            a = CA - 1 - i
            rows = pl.ds(pl.multiple_of((c * CA + a) * LV, LV), LV)
            f = coef[rows, :]
            lw = lam * w
            q = (ysol[rows, :] + lw) * inv_root
            gq[pl.ds(pl.multiple_of(a * LV, LV), LV), :] = q
            return f + lw, fq + f * q

        w, fq = lax.fori_loop(0, CA, cell, (w, fq), unroll=True)
        hi, lo = split(gq[...])
        z = dot3(hi, lo, bhi[...], blo[...], ((1,), (1,)))
        for j in range(NRAD):
            gs[j, pl.ds(c * CA, CA)] = z[:, BR * j : BR * (j + 1)].reshape(CA, LV, BR).astype(WIRE)
        for d in range(1, NRAD):
            back_copy(c, d).start()
        return w, fq

    _, fq = lax.fori_loop(0, NCH, back_chunk, (cr[1], zero))
    part = rz
    for i in range(LV // CA):
        for j in range(NRAD):
            part = part + fq[CA * i : CA * (i + 1), BR * j : BR * (j + 1)]
    acc[pl.ds(CA, CA), :] = part

    total = acc[...]
    base = 0
    for slot, group in enumerate((rad_peers, x_peers, zy_peers)):
        red[slot] = total
        copies = [
            remote(red.at[slot], redr.at[base + i], rss.at[base + i], rrs.at[base + i], peer)
            for i, peer in enumerate(group)
        ]
        for c in copies:
            c.start()
        for i, c in enumerate(copies):
            c.wait_recv()
            total = total + redr[base + i]
        base += len(group)
    alpha = jnp.sum(total[:CA]) / jnp.sum(total[CA:])

    def scale_row(h, carry):
        for f in range(3):
            xb[f, h] = (alpha * mom[f, h]).astype(BF16)
        return carry

    lax.fori_loop(0, NH, scale_row, 0, unroll=4)
    outs = [pltpu.make_async_copy(xb.at[f], out.at[f], out_sem.at[f]) for f in range(3)]
    for o in outs:
        o.start()

    def last_chunk(n, carry):
        c = BA // 16 - 1 - n
        for half_ in range(2):
            cc = 2 * c + 1 - half_
            for d in range(1, NRAD):
                src = lax.rem(rad + NRAD - d, NRAD)
                sl = pl.ds(cc * CA, CA)
                remote(gs.at[src, sl], gr.at[src, sl], gss.at[d, cc], grs.at[d, cc], (az, src)).wait_recv()
        gr[rad, pl.ds(c * 16, 16)] = gs[rad, pl.ds(c * 16, 16)]
        table = inv_tab[...]
        for pair in range(8):
            cols = []
            for i in range(2):
                a = c * 16 + 2 * pair + i
                x = jnp.concatenate([gr[j, a].astype(F32) for j in range(NRAD)], axis=0)
                hi, lo = split(x)
                cols.append(jnp.concatenate([hi, hi, lo], axis=0))
            y = dot(table, jnp.concatenate(cols, axis=1)) * alpha
            for i in range(2):
                pr[pl.ds(2 * pair + i, NH, stride=16), :] = y[:, BR * i : BR * (i + 1)]

        def rows(h, carry):
            xb[3, h, pl.ds(pl.multiple_of(c * 16, 16), 16), :] = pr[pl.ds(pl.multiple_of(h * 16, 16), 16), :].astype(BF16)
            return carry

        lax.fori_loop(0, NH, rows, 0, unroll=8)
        sl = pl.ds(pl.multiple_of(c * 16, 16), 16)
        pltpu.make_async_copy(xb.at[3, :, sl], out.at[3, :, sl], out_sem.at[3 + c]).start()
        return carry

    lax.fori_loop(0, BA // 16, last_chunk, 0)

    for o in outs:
        o.wait()
    for c in range(BA // 16):
        sl = pl.ds(c * 16, 16)
        pltpu.make_async_copy(xb.at[3, :, sl], out.at[3, :, sl], out_sem.at[3 + c]).wait()
    for f, one in halo:
        for c in one:
            c.wait_send()
    for c in (b_mate, b_across, b_relay, c_up, c_dn):
        c.wait_send()
    base = 0
    for slot, group in enumerate((rad_peers, x_peers, zy_peers)):
        for i, peer in enumerate(group):
            remote(red.at[slot], redr.at[base + i], rss.at[base + i], rrs.at[base + i], peer).wait_send()
        base += len(group)

    def drain(c, carry):
        for d in range(1, NRAD):
            fwd_copy(c, d).wait_send()
            back_copy(c, d).wait_send()
        return carry

    lax.fori_loop(0, NCH, drain, 0)


def body(state, source, shear, permeability, radial_basis, radial_eigen):
    fwd_tab, inv_tab = cosine_tables()
    anyspace = pl.BlockSpec(memory_space=pl.ANY)
    vmem = pl.BlockSpec(memory_space=pltpu.VMEM)
    dma = pltpu.SemaphoreType.DMA
    scratch = [
        pltpu.VMEM((7, NH, BA, BR), BF16),
        pltpu.VMEM((6, NH + 2, ROW, BR), F32),
        pltpu.VMEM((6, BA, BR), BF16),
        pltpu.VMEM((6, BA, BR), BF16),
        pltpu.VMEM((6, BA, BR), BF16),
        pltpu.VMEM((6, BA, BR), F32),
        pltpu.VMEM((6, 2, NH, BR), BF16),
        pltpu.VMEM((6, 2, NH, BR), BF16),
        pltpu.VMEM((2, NH, BR), F32),
        pltpu.VMEM((NH * CA, BR), F32),
        pltpu.VMEM((3, NH, BA, BR), F32),
        pltpu.VMEM((NRAD, BA, LV, BR), WIRE),
        pltpu.VMEM((NRAD, BA, LV, BR), WIRE),
        pltpu.VMEM((BA * LV, NM), F32),
        pltpu.VMEM((BA * LV, NM), F32),
        pltpu.VMEM((CA * LV, NM), F32),
        pltpu.VMEM((NRAD, BA, LV, BR), WIRE),
        pltpu.VMEM((NRAD, BA, LV, BR), WIRE),
        pltpu.VMEM((NH * 16, BR), F32),
        pltpu.VMEM((NRAD, BR, NM), F32),
        pltpu.VMEM((NM, NM), BF16),
        pltpu.VMEM((NM, NM), BF16),
        pltpu.VMEM((2, LV, NM), F32),
        pltpu.VMEM((2, LV, NM), F32),
        pltpu.VMEM((2 * CA, BR), F32),
        pltpu.VMEM((3, 2 * CA, BR), F32),
        pltpu.VMEM((13, 2 * CA, BR), F32),
        dma((8,)), dma((8,)),
        dma((6, 2)), dma((6, 2)), dma((6, 2)), dma((6, 2)),
        dma((3,)), dma((3,)),
        dma((NRAD, NCH)), dma((NRAD, NCH)), dma((NRAD, NCH)), dma((NRAD, NCH)),
        dma((2,)), dma((2,)),
        dma((13,)), dma((13,)),
    ]
    return pl.pallas_call(
        kernel,
        out_shape=jax.ShapeDtypeStruct((4, NH, BA, BR), BF16),
        in_specs=[anyspace] * 5 + [vmem] * 3,
        out_specs=anyspace,
        scratch_shapes=scratch,
        compiler_params=pltpu.CompilerParams(
            collective_id=0, has_side_effects=True, vmem_limit_bytes=60 << 20
        ),
        name="residual_step",
    )(state, source, shear, permeability, radial_basis, radial_eigen.reshape(1, NM), fwd_tab, inv_tab)


def solution(mesh):
    placed = (
        P(None, None, "az", "rad"),
        P(None, "az", "rad"),
        P(None, "az", "rad"),
        P(None, "az", "rad"),
        P("rad", None),
        P(),
    )
    return jax.shard_map(
        body, mesh=mesh, in_specs=placed, out_specs=P(None, None, "az", "rad"), check_vma=False
    )
```

```python
import functools
import math

import jax
import jax.numpy as jnp
import numpy as np
from jax import lax
from jax.experimental import pallas as pl
from jax.experimental.pallas import tpu as pltpu
from jax.sharding import PartitionSpec as P

NH = 64
BA = 64
BR = 128
NRAD = 4
NAZ = 32
LV = NH // NRAD
NM = NRAD * BR
CA = 16
NCH = BA // CA
HB = 2
ROW = 80
PAD = 8

BIOT = 2.0
STORAGE = 1.0

F32 = jnp.float32
BF16 = jnp.bfloat16
WIRE = BF16
CODE_SPAN = 152.0
CODE_BASE = 68.0
CODE_ZERO = math.exp(-CODE_BASE)
MESH = pl.DeviceIdType.MESH

ORDER = (3, 5, 0, 1, 2, 4)


def split(x):
    hi = x.astype(BF16)
    lo = (x - hi.astype(F32)).astype(BF16)
    return hi, lo


def encode(x):
    size = jnp.abs(x)
    scale = jnp.maximum(jnp.max(size, axis=0), 1e-30).astype(WIRE)
    rate = CODE_SPAN / scale.astype(F32)
    y = jnp.exp(size * rate[None] - CODE_BASE) - CODE_ZERO
    return jnp.where(x < 0, -y, y).astype(WIRE), scale


def decode(y, scale):
    y = y.astype(F32)
    size = jnp.log(jnp.abs(y) + CODE_ZERO) + CODE_BASE
    return jnp.where(y < 0, -size, size) * (scale.astype(F32) * (1.0 / CODE_SPAN))


def cosine_tables():
    l = np.arange(NH, dtype=np.float64)[:, None]
    h = np.arange(NH, dtype=np.float64)[None, :]
    scale = np.where(l == 0, math.sqrt(1.0 / NH), math.sqrt(2.0 / NH))
    table = jnp.asarray(scale * np.cos(math.pi * (h + 0.5) * l / NH), F32)
    out = []
    for c in (table, table.T):
        hi, lo = split(c)
        out.append(jnp.concatenate([hi, lo, hi], axis=1))
    return out


def remote(src, dst, send, recv, device):
    return pltpu.make_async_remote_copy(
        src_ref=src, dst_ref=dst, send_sem=send, recv_sem=recv,
        device_id=device, device_id_type=MESH,
    )


def dot(a, b, dims=((1,), (0,))):
    return lax.dot_general(a, b, (dims, ((), ())), preferred_element_type=F32)


def dot3(xh, xl, bh, bl, dims):
    return dot(xh, bh, dims) + (dot(xl, bh, dims) + dot(xh, bl, dims))


def kernel(
    state, source, shear, perm, basis, eigen, fwd_tab, inv_tab, out, alpha_ref,
    xb, ext, qs, ql, qr, pk, ahs, ahr, ah32,
    tmp, lev, mom, fs, fr, xh, xl, coef, ysol, gq, gs, gr, pr,
    bas, bhi, blo, cs, cr, acc, red, redr,
    in_sem, out_sem, hs, hr, as_, ar_, bs, br_, fss, frs, gss, grs, css, crs, rss, rrs,
):
    az = lax.axis_index("az")
    rad = lax.axis_index("rad")
    mate = rad + 1 - 2 * lax.rem(rad, 2)
    across = lax.rem(rad + 2, NRAD)
    az_up = lax.rem(az + 1, NAZ)
    az_dn = lax.rem(az + NAZ - 1, NAZ)
    rad_up = lax.rem(rad + 1, NRAD)
    rad_dn = lax.rem(rad + NRAD - 1, NRAD)
    axx = lax.rem(az, 4)
    azy = az // 4
    plane_peers = [
        (azy * 4 + lax.rem(axx + d, 4), lax.rem(rad + e, NRAD))
        for d in range(4) for e in range(NRAD) if d or e
    ]
    zy_peers = [(lax.rem(azy + d, 8) * 4 + axx, rad) for d in range(1, 8)]

    def load(f):
        if f < 4:
            src = state.at[f]
        else:
            src = (shear, perm)[f - 4]
        return pltpu.make_async_copy(src, xb.at[f], in_sem.at[f])

    for f in ORDER:
        load(f).start()
    own_basis = pltpu.make_async_copy(basis, bas.at[rad], in_sem.at[7])
    own_basis.start()
    src_load = pltpu.make_async_copy(source, xb.at[6], in_sem.at[6])
    src_load.start()

    barrier = pltpu.get_barrier_semaphore()
    partners = plane_peers + zy_peers + [(az_up, rad), (az_dn, rad)]
    for peer in partners:
        pl.semaphore_signal(barrier, inc=1, device_id=peer, device_id_type=MESH)
    pl.semaphore_wait(barrier, len(partners))

    b_across = remote(basis, bas.at[rad], bs.at[1], br_.at[1], (az, across))
    b_mate = remote(basis, bas.at[rad], bs.at[0], br_.at[0], (az, mate))
    b_relay = remote(bas.at[across], bas.at[across], bs.at[2], br_.at[2], (az, mate))
    b_across.start()
    b_mate.start()

    lane = lax.broadcasted_iota(jnp.int32, (BA, BR), 1)
    zero_row = jnp.zeros((ROW, BR), F32)
    halo = []
    for n, f in enumerate(ORDER):
        load(f).wait()
        ext[f, 0] = zero_row
        ext[f, NH + 1] = zero_row

        def stage(h, q, f=f):
            x = xb[f, h].astype(F32)
            ext[f, h + 1, pl.ds(PAD, BA), :] = x
            ah32[0, pl.ds(h, 1), :] = x[0:1]
            ah32[1, pl.ds(h, 1), :] = x[BA - 1 : BA]
            rolled = pltpu.roll(x, 2 * h + 1, 1)
            return jnp.where(lane // 2 == h, rolled, q)

        q = lax.fori_loop(0, NH, stage, jnp.zeros((BA, BR), F32), unroll=8)
        qs[f] = q.astype(BF16)
        ahs[f, 0] = ah32[0].astype(BF16)
        ahs[f, 1] = ah32[1].astype(BF16)
        one = [
            remote(qs.at[f], ql.at[f], hs.at[f, 0], hr.at[f, 0], (az, rad_up)),
            remote(qs.at[f], qr.at[f], hs.at[f, 1], hr.at[f, 1], (az, rad_dn)),
            remote(ahs.at[f, 1], ahr.at[f, 0], as_.at[f, 0], ar_.at[f, 0], (az_up, rad)),
            remote(ahs.at[f, 0], ahr.at[f, 1], as_.at[f, 1], ar_.at[f, 1], (az_dn, rad)),
        ]
        for c in one:
            c.start()
        halo.append((f, one))

    even = lax.rem(lane, 2) == 0

    def finish_halo(entry):
        f, one = entry
        for c in one:
            c.wait_recv()
        left = jnp.where(rad > 0, ql[f].astype(F32), 0.0)
        right = jnp.where(rad < NRAD - 1, qr[f].astype(F32), 0.0)
        pk[f] = jnp.where(even, pltpu.roll(right, BR - 1, 1), pltpu.roll(left, 1, 1))
        ah32[0] = ahr[f, 0].astype(F32)
        ah32[1] = ahr[f, 1].astype(F32)

        def place(h, carry):
            ext[f, h + 1, pl.ds(PAD - 1, 1), :] = ah32[0, pl.ds(h, 1), :]
            ext[f, h + 1, pl.ds(PAD + BA, 1), :] = ah32[1, pl.ds(h, 1), :]
            return carry

        lax.fori_loop(0, NH, place, 0, unroll=8)

    def split_basis(j):
        hi, lo = split(bas[j])
        rows = pl.ds(pl.multiple_of(j * BR, BR), BR)
        bhi[rows, :] = hi
        blo[rows, :] = lo

    own_basis.wait()
    split_basis(rad)
    level = (lax.broadcasted_iota(jnp.int32, (LV, NM), 0) + LV * rad).astype(F32)
    half = jnp.sin(level * (math.pi / (2.0 * NH)))
    sigma = STORAGE + eigen[...] + 4.0 * half * half
    root = jnp.sqrt(sigma * (sigma + 4.0))
    lam = 2.0 / (sigma + 2.0 + root)
    inv_root = 1.0 / root
    b_mate.wait_recv()
    split_basis(mate)
    b_across.wait_recv()
    b_relay.start()
    split_basis(across)

    for entry in halo[:5]:
        finish_halo(entry)

    lane3 = lax.broadcasted_iota(jnp.int32, (HB, CA, BR), 2)
    first = lane3 == 0
    last = lane3 == BR - 1

    def block(f, h0, c, dh=0, da=0):
        return ext[f, pl.ds(h0 + 1 + dh, HB), pl.ds(PAD + CA * c + da, CA), :]

    def radial_pair(f, h0, c, v):
        tile = pk[f, pl.ds(pl.multiple_of(CA * c, CA), CA), :]
        ends = jnp.stack([pltpu.roll(tile, 127 - 2 * (h0 + i), 1) for i in range(HB)])
        up = jnp.where(last, ends, pltpu.roll(v, BR - 1, 2))
        down = jnp.where(first, ends, pltpu.roll(v, 1, 2))
        return up, down

    def neighbours(f, h0, c):
        v = block(f, h0, c)
        up, down = radial_pair(f, h0, c, v)
        return v, (
            (block(f, h0, c, dh=1), block(f, h0, c, dh=-1)),
            (block(f, h0, c, da=1), block(f, h0, c, da=-1)),
            (up, down),
        )

    src_load.wait()

    def fluid_chunk(c, rr):
        def rows(b, rr):
            h0 = b * HB
            k, ks = neighbours(5, h0, c)
            p, ps = neighbours(3, h0, c)
            total = jnp.zeros_like(p)
            for axis in range(3):
                for side in range(2):
                    total = total + (k + ks[axis][side]) * (p - ps[axis][side])
            u0 = block(0, h0, c)
            up, down = radial_pair(0, h0, c, u0)
            spread = up - down
            spread = spread + (block(1, h0, c, da=1) - block(1, h0, c, da=-1))
            spread = spread + (block(2, h0, c, dh=1) - block(2, h0, c, dh=-1))
            s = xb[6, pl.ds(h0, HB), pl.ds(pl.multiple_of(CA * c, CA), CA), :].astype(F32)
            res = s + (0.5 * BIOT) * spread + STORAGE * p + 0.5 * total
            tmp[pl.ds(pl.multiple_of(h0 * CA, CA), HB * CA), :] = res.reshape(HB * CA, BR)
            return rr + jnp.sum(res * res, axis=0)

        rr = lax.fori_loop(0, NH // HB, rows, rr, unroll=4)
        table = fwd_tab[...]
        for pair in range(CA // 2):
            cols = []
            for i in range(2):
                x = tmp[pl.ds(2 * pair + i, NH, stride=CA), :]
                hi, lo = split(x)
                cols.append(jnp.concatenate([hi, hi, lo], axis=0))
            y = dot(table, jnp.concatenate(cols, axis=1))
            for i in range(2):
                lev[2 * pair + i] = y[:, BR * i : BR * (i + 1)]
        for d in range(NRAD):
            fs[d, c, pl.ds(0, CA)], fs[d, c, CA] = encode(lev[:, pl.ds(LV * d, LV), :])
        for d in range(1, NRAD):
            fwd_copy(c, d).start()
        return rr

    def fwd_copy(c, d):
        t = lax.rem(rad + d, NRAD)
        return remote(fs.at[t, c], fr.at[rad, c], fss.at[d, c], frs.at[d, c], (az, t))

    rr = lax.fori_loop(0, NCH, fluid_chunk, jnp.zeros((CA, BR), F32))

    finish_halo(halo[5])

    def mom_copy(c):
        sl = pl.ds(pl.multiple_of(CA * c, CA), CA)
        return pltpu.make_async_copy(mom.at[:, :, sl], out.at[pl.ds(0, 3), :, sl], out_sem.at[0, c])

    def moment_chunk(c, carry):
        def rows(b, carry):
            rr, rz = carry
            h0 = b * HB
            g, gs_ = neighbours(4, h0, c)
            face = [[g + gs_[axis][side] for side in range(2)] for axis in range(3)]
            diag2 = (face[0][0] + face[0][1]) + (face[1][0] + face[1][1]) + (face[2][0] + face[2][1])
            p = block(3, h0, c)
            up, down = radial_pair(3, h0, c, p)
            grads = (
                up - down,
                block(3, h0, c, da=1) - block(3, h0, c, da=-1),
                block(3, h0, c, dh=1) - block(3, h0, c, dh=-1),
            )
            inv = 2.0 / diag2
            for f in range(3):
                u, us = neighbours(f, h0, c)
                total = jnp.zeros_like(u)
                for axis in range(3):
                    for side in range(2):
                        total = total + face[axis][side] * (u - us[axis][side])
                res = -(0.5 * total + (0.5 * BIOT) * grads[f])
                step = res * inv
                mom[f, pl.ds(h0, HB), pl.ds(pl.multiple_of(CA * c, CA), CA), :] = step
                rr = rr + jnp.sum(res * res, axis=0)
                rz = rz + jnp.sum(res * step, axis=0)
            return rr, rz

        carry = lax.fori_loop(0, NH // HB, rows, carry, unroll=4)
        mom_copy(c).start()
        return carry

    rr, rz = lax.fori_loop(0, NCH, moment_chunk, (rr, jnp.zeros((CA, BR), F32)))
    acc[pl.ds(0, CA), :] = rr

    b_relay.wait_recv()
    split_basis(mate + 2 - 4 * (mate // 2))

    def fwd_chunk(c, carry):
        y, w, power = carry
        for d in range(1, NRAD):
            src = lax.rem(rad + NRAD - d, NRAD)
            remote(fs.at[src, c], fr.at[src, c], fss.at[d, c], frs.at[d, c], (az, src)).wait_recv()
        fr[rad, c] = fs[rad, c]
        for j in range(NRAD):
            scale = fr[j, c, CA]
            for i in range(0, CA, 4):
                x = decode(fr[j, c, pl.ds(i, 4)], scale).reshape(4 * LV, BR)
                hi, lo = split(x)
                xh[pl.ds(i * LV, 4 * LV), pl.ds(j * BR, BR)] = hi
                xl[pl.ds(i * LV, 4 * LV), pl.ds(j * BR, BR)] = lo
        z = dot3(xh[...], xl[...], bhi[...], blo[...], ((1,), (0,)))
        coef[pl.ds(pl.multiple_of(c * CA * LV, CA * LV), CA * LV), :] = z
        for i in range(CA):
            f = z[i * LV : (i + 1) * LV]
            y = lam * y + f
            w = w + power * f
            power = power * lam
        return y, w, power

    zero = jnp.zeros((LV, NM), F32)
    y, w, _ = lax.fori_loop(0, NCH, fwd_chunk, (zero, zero, jnp.ones((LV, NM), F32)))
    cs[0] = y
    cs[1] = w
    c_up = remote(cs.at[0], cr.at[0], css.at[0], crs.at[0], (az_up, rad))
    c_dn = remote(cs.at[1], cr.at[1], css.at[1], crs.at[1], (az_dn, rad))
    c_up.start()
    c_dn.start()
    c_up.wait_recv()

    def sweep_up(a, y):
        rows = pl.ds(pl.multiple_of(a * LV, LV), LV)
        y = lam * y + coef[rows, :]
        ysol[rows, :] = y
        return y

    lax.fori_loop(0, BA, sweep_up, cr[0], unroll=8)
    c_dn.wait_recv()

    def back_copy(c, d):
        t = lax.rem(rad + d, NRAD)
        return remote(gs.at[t, c], gr.at[rad, c], gss.at[d, c], grs.at[d, c], (az, t))

    def back_chunk(n, carry):
        w, fq = carry
        c = NCH - 1 - n

        def cell(i, carry):
            w, fq = carry
            a = CA - 1 - i
            rows = pl.ds(pl.multiple_of((c * CA + a) * LV, LV), LV)
            f = coef[rows, :]
            lw = lam * w
            q = (ysol[rows, :] + lw) * inv_root
            gq[pl.ds(pl.multiple_of(a * LV, LV), LV), :] = q
            return f + lw, fq + f * q

        w, fq = lax.fori_loop(0, CA, cell, (w, fq), unroll=True)
        hi, lo = split(gq[...])
        z = dot3(hi, lo, bhi[...], blo[...], ((1,), (1,)))
        for j in range(NRAD):
            gs[j, c, pl.ds(0, CA)], gs[j, c, CA] = encode(z[:, BR * j : BR * (j + 1)].reshape(CA, LV, BR))
        for d in range(1, NRAD):
            back_copy(c, d).start()
        return w, fq

    _, fq = lax.fori_loop(0, NCH, back_chunk, (cr[1], zero))
    part = rz
    for j in range(NRAD):
        part = part + fq[:, BR * j : BR * (j + 1)]
    acc[pl.ds(CA, CA), :] = part

    def reduce_copies(slot):
        group, base = ((plane_peers, 0), (zy_peers, len(plane_peers)))[slot]
        return [
            remote(red.at[slot], redr.at[base + i], rss.at[base + i], rrs.at[base + i], peer)
            for i, peer in enumerate(group)
        ], base

    def reduce_finish(slot, total):
        copies, base = reduce_copies(slot)
        for i, c in enumerate(copies):
            c.wait_recv()
            total = total + redr[base + i]
        return total

    def press_copy(c):
        sl = pl.ds(pl.multiple_of(CA * c, CA), CA)
        return pltpu.make_async_copy(pr.at[c], out.at[3, :, sl], out_sem.at[1, c])

    def last_chunk(n, carry):
        c = NCH - 1 - n
        for d in range(1, NRAD):
            src = lax.rem(rad + NRAD - d, NRAD)
            remote(gs.at[src, c], gr.at[src, c], gss.at[d, c], grs.at[d, c], (az, src)).wait_recv()
        gr[rad, c] = gs[rad, c]
        table = inv_tab[...]
        rows = pr.at[c].reshape(NH * CA, BR)
        for pair in range(CA // 2):
            cols = []
            for i in range(2):
                a = 2 * pair + i
                x = jnp.concatenate([decode(gr[j, c, a], gr[j, c, CA]) for j in range(NRAD)], axis=0)
                hi, lo = split(x)
                cols.append(jnp.concatenate([hi, hi, lo], axis=0))
            y = dot(table, jnp.concatenate(cols, axis=1))
            for i in range(2):
                rows[pl.ds(2 * pair + i, NH, stride=CA), :] = y[:, BR * i : BR * (i + 1)]
        press_copy(c).start()
        return carry

    red[0] = acc[...]
    for c in reduce_copies(0)[0]:
        c.start()
    last_chunk(0, 0)
    total = reduce_finish(0, acc[...])
    red[1] = total
    for c in reduce_copies(1)[0]:
        c.start()
    lax.fori_loop(1, NCH, last_chunk, 0)
    total = reduce_finish(1, total)
    alpha_ref[0, 0] = jnp.sum(total[:CA]) / jnp.sum(total[CA:])

    for f, one in halo:
        for c in one:
            c.wait_send()
    for c in (b_mate, b_across, b_relay, c_up, c_dn):
        c.wait_send()
    for slot in range(2):
        for c in reduce_copies(slot)[0]:
            c.wait_send()

    def drain(c, carry):
        for d in range(1, NRAD):
            fwd_copy(c, d).wait_send()
            back_copy(c, d).wait_send()
        mom_copy(c).wait()
        press_copy(c).wait()
        return carry

    lax.fori_loop(0, NCH, drain, 0)


def body(state, source, shear, permeability, radial_basis, radial_eigen):
    fwd_tab, inv_tab = cosine_tables()
    anyspace = pl.BlockSpec(memory_space=pl.ANY)
    vmem = pl.BlockSpec(memory_space=pltpu.VMEM)
    dma = pltpu.SemaphoreType.DMA
    scratch = [
        pltpu.VMEM((7, NH, BA, BR), BF16),
        pltpu.VMEM((6, NH + 2, ROW, BR), F32),
        pltpu.VMEM((6, BA, BR), BF16),
        pltpu.VMEM((6, BA, BR), BF16),
        pltpu.VMEM((6, BA, BR), BF16),
        pltpu.VMEM((6, BA, BR), F32),
        pltpu.VMEM((6, 2, NH, BR), BF16),
        pltpu.VMEM((6, 2, NH, BR), BF16),
        pltpu.VMEM((2, NH, BR), F32),
        pltpu.VMEM((NH * CA, BR), F32),
        pltpu.VMEM((CA, NH, BR), F32),
        pltpu.VMEM((3, NH, BA, BR), F32),
        pltpu.VMEM((NRAD, NCH, CA + 1, LV, BR), WIRE),
        pltpu.VMEM((NRAD, NCH, CA + 1, LV, BR), WIRE),
        pltpu.VMEM((CA * LV, NM), BF16),
        pltpu.VMEM((CA * LV, NM), BF16),
        pltpu.VMEM((BA * LV, NM), F32),
        pltpu.VMEM((BA * LV, NM), F32),
        pltpu.VMEM((CA * LV, NM), F32),
        pltpu.VMEM((NRAD, NCH, CA + 1, LV, BR), WIRE),
        pltpu.VMEM((NRAD, NCH, CA + 1, LV, BR), WIRE),
        pltpu.VMEM((NCH, NH, CA, BR), F32),
        pltpu.VMEM((NRAD, BR, NM), F32),
        pltpu.VMEM((NM, NM), BF16),
        pltpu.VMEM((NM, NM), BF16),
        pltpu.VMEM((2, LV, NM), F32),
        pltpu.VMEM((2, LV, NM), F32),
        pltpu.VMEM((2 * CA, BR), F32),
        pltpu.VMEM((2, 2 * CA, BR), F32),
        pltpu.VMEM((22, 2 * CA, BR), F32),
        dma((8,)), dma((2, NCH)),
        dma((6, 2)), dma((6, 2)), dma((6, 2)), dma((6, 2)),
        dma((3,)), dma((3,)),
        dma((NRAD, NCH)), dma((NRAD, NCH)), dma((NRAD, NCH)), dma((NRAD, NCH)),
        dma((2,)), dma((2,)),
        dma((22,)), dma((22,)),
    ]
    step, alpha = pl.pallas_call(
        kernel,
        out_shape=(jax.ShapeDtypeStruct((4, NH, BA, BR), F32), jax.ShapeDtypeStruct((1, 1), F32)),
        in_specs=[anyspace] * 5 + [vmem] * 3,
        out_specs=(anyspace, pl.BlockSpec(memory_space=pltpu.SMEM)),
        scratch_shapes=scratch,
        compiler_params=pltpu.CompilerParams(
            collective_id=0, has_side_effects=True, vmem_limit_bytes=60 << 20
        ),
        name="residual_step",
    )(state, source, shear, permeability, radial_basis, radial_eigen.reshape(1, NM), fwd_tab, inv_tab)
    return (alpha[0, 0] * step).astype(BF16)


def solution(mesh):
    placed = (
        P(None, None, "az", "rad"),
        P(None, "az", "rad"),
        P(None, "az", "rad"),
        P(None, "az", "rad"),
        P("rad", None),
        P(),
    )
    return jax.shard_map(
        body, mesh=mesh, in_specs=placed, out_specs=P(None, None, "az", "rad"), check_vma=False
    )
```

```python
import functools
import math

import jax
import jax.numpy as jnp
import numpy as np
from jax import lax
from jax.experimental import pallas as pl
from jax.experimental.pallas import tpu as pltpu
from jax.sharding import PartitionSpec as P

NH = 64
BA = 64
BR = 128
NRAD = 4
NAZ = 32
LV = NH // NRAD
NM = NRAD * BR
CA = 16
NCH = BA // CA
HB = 2
ROW = 80
PAD = 8
EARLY = 2

BIOT = 2.0
STORAGE = 1.0

F32 = jnp.float32
BF16 = jnp.bfloat16
WIRE = BF16
CODE_SPAN = 152.0
CODE_BASE = 68.0
CODE_ZERO = math.exp(-CODE_BASE)
MESH = pl.DeviceIdType.MESH

ORDER = (3, 5, 0, 1, 2, 4)


def split(x):
    hi = x.astype(BF16)
    lo = (x - hi.astype(F32)).astype(BF16)
    return hi, lo


def encode(x):
    size = jnp.abs(x)
    scale = jnp.maximum(jnp.max(size, axis=0), 1e-30).astype(WIRE)
    rate = CODE_SPAN / scale.astype(F32)
    y = jnp.exp(size * rate[None] - CODE_BASE) - CODE_ZERO
    return jnp.where(x < 0, -y, y).astype(WIRE), scale


def decode(y, scale):
    y = y.astype(F32)
    size = jnp.log(jnp.abs(y) + CODE_ZERO) + CODE_BASE
    return jnp.where(y < 0, -size, size) * (scale.astype(F32) * (1.0 / CODE_SPAN))


def cosine_tables():
    l = np.arange(NH, dtype=np.float64)[:, None]
    h = np.arange(NH, dtype=np.float64)[None, :]
    scale = np.where(l == 0, math.sqrt(1.0 / NH), math.sqrt(2.0 / NH))
    table = jnp.asarray(scale * np.cos(math.pi * (h + 0.5) * l / NH), F32)
    out = []
    for c in (table, table.T):
        hi, lo = split(c)
        out.append(jnp.concatenate([hi, lo, hi], axis=1))
    return out


def remote(src, dst, send, recv, device):
    return pltpu.make_async_remote_copy(
        src_ref=src, dst_ref=dst, send_sem=send, recv_sem=recv,
        device_id=device, device_id_type=MESH,
    )


def dot(a, b, dims=((1,), (0,))):
    return lax.dot_general(a, b, (dims, ((), ())), preferred_element_type=F32)


def dot3(xh, xl, bh, bl, dims):
    return dot(xh, bh, dims) + (dot(xl, bh, dims) + dot(xh, bl, dims))


def kernel(
    state, source, shear, perm, basis, eigen, fwd_tab, inv_tab, out, alpha_ref,
    xb, ext, qs, ql, qr, pk, ahs, ahr, ah32,
    tmp, lev, fs, fr, xh, xl, coef, ysol, gq, gs, gr,
    bas, bhi, blo, cs, cr, acc, red, redr,
    in_sem, hs, hr, as_, ar_, bs, br_, fss, frs, gss, grs, css, crs, rss, rrs,
):
    az = lax.axis_index("az")
    rad = lax.axis_index("rad")
    mate = rad + 1 - 2 * lax.rem(rad, 2)
    across = lax.rem(rad + 2, NRAD)
    az_up = lax.rem(az + 1, NAZ)
    az_dn = lax.rem(az + NAZ - 1, NAZ)
    rad_up = lax.rem(rad + 1, NRAD)
    rad_dn = lax.rem(rad + NRAD - 1, NRAD)
    axx = lax.rem(az, 4)
    azy = az // 4
    near_peers = [
        ((azy // 2) * 8 + lax.rem(azy + d, 2) * 4 + axx, lax.rem(rad + e, NRAD))
        for d in range(2) for e in range(NRAD) if d or e
    ]
    far_peers = [
        ((lax.rem(azy // 2 + d, 4) * 2 + lax.rem(azy, 2)) * 4 + lax.rem(axx + e, 4), rad)
        for d in range(4) for e in range(4) if d or e
    ]

    def load(f):
        if f < 4:
            src = state.at[f]
        else:
            src = (shear, perm)[f - 4]
        return pltpu.make_async_copy(src, xb.at[f], in_sem.at[f])

    for f in ORDER:
        load(f).start()
    own_basis = pltpu.make_async_copy(basis, bas.at[rad], in_sem.at[7])
    own_basis.start()
    src_load = pltpu.make_async_copy(source, xb.at[6], in_sem.at[6])
    src_load.start()

    barrier = pltpu.get_barrier_semaphore()
    partners = near_peers + far_peers + [(az_up, rad), (az_dn, rad)]
    for peer in partners:
        pl.semaphore_signal(barrier, inc=1, device_id=peer, device_id_type=MESH)
    pl.semaphore_wait(barrier, len(partners))

    lane = lax.broadcasted_iota(jnp.int32, (BA, BR), 1)
    zero_row = jnp.zeros((ROW, BR), F32)
    halo = {}
    def stage_field(f):
        load(f).wait()
        ext[f, 0] = zero_row
        ext[f, NH + 1] = zero_row

        def stage(h, q, f=f):
            x = xb[f, h].astype(F32)
            ext[f, h + 1, pl.ds(PAD, BA), :] = x
            ah32[0, pl.ds(h, 1), :] = x[0:1]
            ah32[1, pl.ds(h, 1), :] = x[BA - 1 : BA]
            rolled = pltpu.roll(x, 2 * h + 1, 1)
            return jnp.where(lane // 2 == h, rolled, q)

        q = lax.fori_loop(0, NH, stage, jnp.zeros((BA, BR), F32), unroll=8)
        qs[f] = q.astype(BF16)
        ahs[f, 0] = ah32[0].astype(BF16)
        ahs[f, 1] = ah32[1].astype(BF16)
        one = [
            remote(qs.at[f], ql.at[f], hs.at[f, 0], hr.at[f, 0], (az, rad_up)),
            remote(qs.at[f], qr.at[f], hs.at[f, 1], hr.at[f, 1], (az, rad_dn)),
            remote(ahs.at[f, 1], ahr.at[f, 0], as_.at[f, 0], ar_.at[f, 0], (az_up, rad)),
            remote(ahs.at[f, 0], ahr.at[f, 1], as_.at[f, 1], ar_.at[f, 1], (az_dn, rad)),
        ]
        for c in one:
            c.start()
        halo[f] = one

    for f in ORDER[:5]:
        stage_field(f)

    b_across = remote(basis, bas.at[rad], bs.at[1], br_.at[1], (az, across))
    b_mate = remote(basis, bas.at[rad], bs.at[0], br_.at[0], (az, mate))
    b_relay = remote(bas.at[across], bas.at[across], bs.at[2], br_.at[2], (az, mate))
    b_across.start()
    b_mate.start()

    even = lax.rem(lane, 2) == 0

    def finish_halo(f):
        for c in halo[f]:
            c.wait_recv()
        left = jnp.where(rad > 0, ql[f].astype(F32), 0.0)
        right = jnp.where(rad < NRAD - 1, qr[f].astype(F32), 0.0)
        pk[f] = jnp.where(even, pltpu.roll(right, BR - 1, 1), pltpu.roll(left, 1, 1))
        ah32[0] = ahr[f, 0].astype(F32)
        ah32[1] = ahr[f, 1].astype(F32)

        def place(h, carry):
            ext[f, h + 1, pl.ds(PAD - 1, 1), :] = ah32[0, pl.ds(h, 1), :]
            ext[f, h + 1, pl.ds(PAD + BA, 1), :] = ah32[1, pl.ds(h, 1), :]
            return carry

        lax.fori_loop(0, NH, place, 0, unroll=8)

    def split_basis(j):
        hi, lo = split(bas[j])
        rows = pl.ds(pl.multiple_of(j * BR, BR), BR)
        bhi[rows, :] = hi
        blo[rows, :] = lo

    own_basis.wait()
    split_basis(rad)
    level = (lax.broadcasted_iota(jnp.int32, (LV, NM), 0) + LV * rad).astype(F32)
    half = jnp.sin(level * (math.pi / (2.0 * NH)))
    sigma = STORAGE + eigen[...] + 4.0 * half * half
    root = jnp.sqrt(sigma * (sigma + 4.0))
    lam = 2.0 / (sigma + 2.0 + root)
    inv_root = 1.0 / root
    for f in ORDER[:4]:
        finish_halo(f)

    lane3 = lax.broadcasted_iota(jnp.int32, (HB, CA, BR), 2)
    first = lane3 == 0
    last = lane3 == BR - 1

    def block(f, h0, c, dh=0, da=0):
        return ext[f, pl.ds(h0 + 1 + dh, HB), pl.ds(PAD + CA * c + da, CA), :]

    def radial_pair(f, h0, c, v):
        tile = pk[f, pl.ds(pl.multiple_of(CA * c, CA), CA), :]
        ends = jnp.stack([pltpu.roll(tile, 127 - 2 * (h0 + i), 1) for i in range(HB)])
        up = jnp.where(last, ends, pltpu.roll(v, BR - 1, 2))
        down = jnp.where(first, ends, pltpu.roll(v, 1, 2))
        return up, down

    def neighbours(f, h0, c):
        v = block(f, h0, c)
        up, down = radial_pair(f, h0, c, v)
        return v, (
            (block(f, h0, c, dh=1), block(f, h0, c, dh=-1)),
            (block(f, h0, c, da=1), block(f, h0, c, da=-1)),
            (up, down),
        )

    src_load.wait()

    def fluid_chunk(c, rr):
        def rows(b, rr):
            h0 = b * HB
            k, ks = neighbours(5, h0, c)
            p, ps = neighbours(3, h0, c)
            total = jnp.zeros_like(p)
            for axis in range(3):
                for side in range(2):
                    total = total + (k + ks[axis][side]) * (p - ps[axis][side])
            u0 = block(0, h0, c)
            up, down = radial_pair(0, h0, c, u0)
            spread = up - down
            spread = spread + (block(1, h0, c, da=1) - block(1, h0, c, da=-1))
            spread = spread + (block(2, h0, c, dh=1) - block(2, h0, c, dh=-1))
            s = xb[6, pl.ds(h0, HB), pl.ds(pl.multiple_of(CA * c, CA), CA), :].astype(F32)
            res = s + (0.5 * BIOT) * spread + STORAGE * p + 0.5 * total
            tmp[pl.ds(pl.multiple_of(h0 * CA, CA), HB * CA), :] = res.reshape(HB * CA, BR)
            return rr + jnp.sum(res * res, axis=0)

        rr = lax.fori_loop(0, NH // HB, rows, rr, unroll=4)
        table = fwd_tab[...]
        for pair in range(CA // 2):
            cols = []
            for i in range(2):
                x = tmp[pl.ds(2 * pair + i, NH, stride=CA), :]
                hi, lo = split(x)
                cols.append(jnp.concatenate([hi, hi, lo], axis=0))
            y = dot(table, jnp.concatenate(cols, axis=1))
            for i in range(2):
                lev[2 * pair + i] = y[:, BR * i : BR * (i + 1)]
        for d in range(NRAD):
            fs[d, c, pl.ds(0, CA)], fs[d, c, CA] = encode(lev[:, pl.ds(LV * d, LV), :])
        for d in range(1, NRAD):
            fwd_copy(c, d).start()
        return rr

    def fwd_copy(c, d):
        t = lax.rem(rad + d, NRAD)
        return remote(fs.at[t, c], fr.at[rad, c], fss.at[d, c], frs.at[d, c], (az, t))

    rr = lax.fori_loop(0, NCH // 2, fluid_chunk, jnp.zeros((CA, BR), F32))
    stage_field(ORDER[5])
    b_mate.wait_recv()
    split_basis(mate)
    b_across.wait_recv()
    b_relay.start()
    split_basis(across)
    rr = lax.fori_loop(NCH // 2, NCH, fluid_chunk, rr)

    for f in ORDER[4:]:
        finish_halo(f)

    def moment_chunk(c, carry):
        def rows(b, carry):
            rr, rz = carry
            h0 = b * HB
            g, gs_ = neighbours(4, h0, c)
            face = [[g + gs_[axis][side] for side in range(2)] for axis in range(3)]
            diag2 = (face[0][0] + face[0][1]) + (face[1][0] + face[1][1]) + (face[2][0] + face[2][1])
            p = block(3, h0, c)
            up, down = radial_pair(3, h0, c, p)
            grads = (
                up - down,
                block(3, h0, c, da=1) - block(3, h0, c, da=-1),
                block(3, h0, c, dh=1) - block(3, h0, c, dh=-1),
            )
            inv = 1.0 / diag2
            square = jnp.zeros_like(p)
            for f in range(3):
                u, us = neighbours(f, h0, c)
                res = -BIOT * grads[f] - diag2 * u
                for axis in range(3):
                    for side in range(2):
                        res = res + face[axis][side] * us[axis][side]
                step = res * inv
                for i in range(HB):
                    out[pl.ds(pl.multiple_of((f * NH + h0 + i) * BA + CA * c, CA), CA), :] = step[i]
                square = square + res * res
            return rr + jnp.sum(square, axis=0), rz + jnp.sum(square * inv, axis=0)

        return lax.fori_loop(0, NH // HB, rows, carry, unroll=4)

    quad = jnp.zeros((CA, BR), F32)
    quad = lax.fori_loop(0, EARLY, moment_chunk, (quad, quad))

    b_relay.wait_recv()
    split_basis(mate + 2 - 4 * (mate // 2))

    def fwd_chunk(c, carry):
        y, w, power = carry
        for d in range(1, NRAD):
            src = lax.rem(rad + NRAD - d, NRAD)
            remote(fs.at[src, c], fr.at[src, c], fss.at[d, c], frs.at[d, c], (az, src)).wait_recv()
        fr[rad, c] = fs[rad, c]
        for j in range(NRAD):
            scale = fr[j, c, CA]
            for i in range(0, CA, 4):
                x = decode(fr[j, c, pl.ds(i, 4)], scale).reshape(4 * LV, BR)
                hi, lo = split(x)
                xh[pl.ds(i * LV, 4 * LV), pl.ds(j * BR, BR)] = hi
                xl[pl.ds(i * LV, 4 * LV), pl.ds(j * BR, BR)] = lo
        z = dot3(xh[...], xl[...], bhi[...], blo[...], ((1,), (0,)))
        coef[pl.ds(pl.multiple_of(c * CA * LV, CA * LV), CA * LV), :] = z
        for i in range(CA):
            f = z[i * LV : (i + 1) * LV]
            y = lam * y + f
            w = w + power * f
            power = power * lam
        return y, w, power

    zero = jnp.zeros((LV, NM), F32)
    y, w, _ = lax.fori_loop(0, NCH, fwd_chunk, (zero, zero, jnp.ones((LV, NM), F32)))
    cs[0] = y
    cs[1] = w
    c_up = remote(cs.at[0], cr.at[0], css.at[0], crs.at[0], (az_up, rad))
    c_dn = remote(cs.at[1], cr.at[1], css.at[1], crs.at[1], (az_dn, rad))
    c_up.start()
    c_dn.start()
    quad = lax.fori_loop(EARLY, NCH, moment_chunk, quad)
    acc[pl.ds(0, CA), :] = rr + 0.25 * quad[0]
    c_up.wait_recv()

    def sweep_up(a, carry):
        y, yy = carry
        rows = pl.ds(pl.multiple_of(a * LV, LV), LV)
        y = lam * y + coef[rows, :]
        ysol[rows, :] = y
        return y, yy + y * y

    _, yy = lax.fori_loop(0, BA, sweep_up, (cr[0], zero), unroll=8)
    yy = lam * yy
    part = 0.5 * quad[1]
    for j in range(NRAD):
        part = part + yy[:, BR * j : BR * (j + 1)]
    acc[pl.ds(CA, CA), :] = part

    def reduce_copies(slot):
        group, base = ((near_peers, 0), (far_peers, len(near_peers)))[slot]
        return [
            remote(red.at[slot], redr.at[base + i], rss.at[base + i], rrs.at[base + i], peer)
            for i, peer in enumerate(group)
        ], base

    def reduce_finish(slot, total):
        copies, base = reduce_copies(slot)
        for i, c in enumerate(copies):
            c.wait_recv()
            total = total + redr[base + i]
        return total

    red[0] = acc[...]
    for c in reduce_copies(0)[0]:
        c.start()
    c_dn.wait_recv()

    def back_copy(c, d):
        t = lax.rem(rad + d, NRAD)
        return remote(gs.at[t, c], gr.at[rad, c], gss.at[d, c], grs.at[d, c], (az, t))

    def back_chunk(n, w):
        c = NCH - 1 - n

        def cell(i, w):
            a = CA - 1 - i
            rows = pl.ds(pl.multiple_of((c * CA + a) * LV, LV), LV)
            f = coef[rows, :]
            lw = lam * w
            q = (ysol[rows, :] + lw) * inv_root
            gq[pl.ds(pl.multiple_of(a * LV, LV), LV), :] = q
            return f + lw

        w = lax.fori_loop(0, CA, cell, w, unroll=True)
        hi, lo = split(gq[...])
        z = dot3(hi, lo, bhi[...], blo[...], ((1,), (1,)))
        for j in range(NRAD):
            gs[j, c, pl.ds(0, CA)], gs[j, c, CA] = encode(z[:, BR * j : BR * (j + 1)].reshape(CA, LV, BR))
        for d in range(1, NRAD):
            back_copy(c, d).start()
        return w

    lax.fori_loop(0, NCH, back_chunk, cr[1])
    def last_chunk(n, carry):
        c = NCH - 1 - n
        for d in range(1, NRAD):
            src = lax.rem(rad + NRAD - d, NRAD)
            remote(gs.at[src, c], gr.at[src, c], gss.at[d, c], grs.at[d, c], (az, src)).wait_recv()
        gr[rad, c] = gs[rad, c]
        table = inv_tab[...]
        for pair in range(CA // 2):
            cols = []
            for i in range(2):
                a = 2 * pair + i
                x = jnp.concatenate([decode(gr[j, c, a], gr[j, c, CA]) for j in range(NRAD)], axis=0)
                hi, lo = split(x)
                cols.append(jnp.concatenate([hi, hi, lo], axis=0))
            y = dot(table, jnp.concatenate(cols, axis=1))
            for i in range(2):
                out[pl.ds(3 * NH * BA + c * CA + 2 * pair + i, NH, stride=BA), :] = y[:, BR * i : BR * (i + 1)]
        return carry

    total = reduce_finish(0, acc[...])
    red[1] = total
    for c in reduce_copies(1)[0]:
        c.start()
    lax.fori_loop(0, NCH, last_chunk, 0)
    total = reduce_finish(1, total)
    alpha_ref[0, 0] = jnp.sum(total[:CA]) / jnp.sum(total[CA:])

    for one in halo.values():
        for c in one:
            c.wait_send()
    for c in (b_mate, b_across, b_relay, c_up, c_dn):
        c.wait_send()
    for slot in range(2):
        for c in reduce_copies(slot)[0]:
            c.wait_send()

    def drain(c, carry):
        for d in range(1, NRAD):
            fwd_copy(c, d).wait_send()
            back_copy(c, d).wait_send()
        return carry

    lax.fori_loop(0, NCH, drain, 0)


def body(state, source, shear, permeability, radial_basis, radial_eigen):
    fwd_tab, inv_tab = cosine_tables()
    anyspace = pl.BlockSpec(memory_space=pltpu.HBM)
    vmem = pl.BlockSpec(memory_space=pltpu.VMEM)
    dma = pltpu.SemaphoreType.DMA
    scratch = [
        pltpu.VMEM((7, NH, BA, BR), BF16),
        pltpu.VMEM((6, NH + 2, ROW, BR), F32),
        pltpu.VMEM((6, BA, BR), BF16),
        pltpu.VMEM((6, BA, BR), BF16),
        pltpu.VMEM((6, BA, BR), BF16),
        pltpu.VMEM((6, BA, BR), F32),
        pltpu.VMEM((6, 2, NH, BR), BF16),
        pltpu.VMEM((6, 2, NH, BR), BF16),
        pltpu.VMEM((2, NH, BR), F32),
        pltpu.VMEM((NH * CA, BR), F32),
        pltpu.VMEM((CA, NH, BR), F32),
        pltpu.VMEM((NRAD, NCH, CA + 1, LV, BR), WIRE),
        pltpu.VMEM((NRAD, NCH, CA + 1, LV, BR), WIRE),
        pltpu.VMEM((CA * LV, NM), BF16),
        pltpu.VMEM((CA * LV, NM), BF16),
        pltpu.VMEM((BA * LV, NM), F32),
        pltpu.VMEM((BA * LV, NM), F32),
        pltpu.VMEM((CA * LV, NM), F32),
        pltpu.VMEM((NRAD, NCH, CA + 1, LV, BR), WIRE),
        pltpu.VMEM((NRAD, NCH, CA + 1, LV, BR), WIRE),
        pltpu.VMEM((NRAD, BR, NM), F32),
        pltpu.VMEM((NM, NM), BF16),
        pltpu.VMEM((NM, NM), BF16),
        pltpu.VMEM((2, LV, NM), F32),
        pltpu.VMEM((2, LV, NM), F32),
        pltpu.VMEM((2 * CA, BR), F32),
        pltpu.VMEM((2, 2 * CA, BR), F32),
        pltpu.VMEM((22, 2 * CA, BR), F32),
        dma((8,)),
        dma((6, 2)), dma((6, 2)), dma((6, 2)), dma((6, 2)),
        dma((3,)), dma((3,)),
        dma((NRAD, NCH)), dma((NRAD, NCH)), dma((NRAD, NCH)), dma((NRAD, NCH)),
        dma((2,)), dma((2,)),
        dma((22,)), dma((22,)),
    ]
    step, alpha = pl.pallas_call(
        kernel,
        out_shape=(pltpu.VMEM((4 * NH * BA, BR), F32), jax.ShapeDtypeStruct((1, 1), F32)),
        in_specs=[anyspace] * 5 + [vmem] * 3,
        out_specs=(vmem, pl.BlockSpec(memory_space=pltpu.SMEM)),
        scratch_shapes=scratch,
        compiler_params=pltpu.CompilerParams(
            collective_id=0, has_side_effects=True, vmem_limit_bytes=52 << 20
        ),
        name="residual_step",
    )(state, source, shear, permeability, radial_basis, radial_eigen.reshape(1, NM), fwd_tab, inv_tab)
    return (alpha[0, 0] * step).astype(BF16).reshape(4, NH, BA, BR)


def solution(mesh):
    placed = (
        P(None, None, "az", "rad"),
        P(None, "az", "rad"),
        P(None, "az", "rad"),
        P(None, "az", "rad"),
        P("rad", None),
        P(),
    )
    return jax.shard_map(
        body, mesh=mesh, in_specs=placed, out_specs=P(None, None, "az", "rad"), check_vma=False
    )
```

```python
import functools
import math

import jax
import jax.numpy as jnp
import numpy as np
from jax import lax
from jax.experimental import pallas as pl
from jax.experimental.pallas import tpu as pltpu
from jax.sharding import PartitionSpec as P

NH = 64
BA = 64
BR = 128
NRAD = 4
NAZ = 32
LV = NH // NRAD
NM = NRAD * BR
CA = 16
NCH = BA // CA
HB = 2
ROW = 80
PAD = 8
EARLY = 2

BIOT = 2.0
STORAGE = 1.0

F32 = jnp.float32
BF16 = jnp.bfloat16
WIRE = BF16
CODE_SPAN = 152.0
CODE_BASE = 68.0
CODE_ZERO = math.exp(-CODE_BASE)
MESH = pl.DeviceIdType.MESH

ORDER = (3, 5, 0, 1, 2, 4)


def split(x):
    hi = x.astype(BF16)
    lo = (x - hi.astype(F32)).astype(BF16)
    return hi, lo


def encode(x):
    size = jnp.abs(x)
    scale = jnp.maximum(jnp.max(size, axis=0), 1e-30).astype(WIRE)
    rate = CODE_SPAN / scale.astype(F32)
    y = jnp.exp(size * rate[None] - CODE_BASE) - CODE_ZERO
    return jnp.where(x < 0, -y, y).astype(WIRE), scale


def decode(y, scale):
    y = y.astype(F32)
    size = jnp.log(jnp.abs(y) + CODE_ZERO) + CODE_BASE
    return jnp.where(y < 0, -size, size) * (scale.astype(F32) * (1.0 / CODE_SPAN))


def cosine_tables():
    l = np.arange(NH, dtype=np.float64)[:, None]
    h = np.arange(NH, dtype=np.float64)[None, :]
    scale = np.where(l == 0, math.sqrt(1.0 / NH), math.sqrt(2.0 / NH))
    table = jnp.asarray(scale * np.cos(math.pi * (h + 0.5) * l / NH), F32)
    out = []
    for c in (table, table.T):
        hi, lo = split(c)
        out.append(jnp.concatenate([hi, lo, hi], axis=1))
    return out


def remote(src, dst, send, recv, device):
    return pltpu.make_async_remote_copy(
        src_ref=src, dst_ref=dst, send_sem=send, recv_sem=recv,
        device_id=device, device_id_type=MESH,
    )


def dot(a, b, dims=((1,), (0,))):
    return lax.dot_general(a, b, (dims, ((), ())), preferred_element_type=F32)


def dot3(xh, xl, bh, bl, dims):
    return dot(xh, bh, dims) + (dot(xl, bh, dims) + dot(xh, bl, dims))


def kernel(
    state, source, shear, perm, basis, eigen, fwd_tab, inv_tab, out, alpha_ref,
    xb, ext, qs, ql, qr, pk, ahs, ahr, ah32,
    tmp, cor, lev, fs, fr, xh, xl, coef, ysol, gq, gs, gr,
    own, code, bas, bhi, blo, cs, cr, acc, red, redr,
    in_sem, hs, hr, as_, ar_, bs, br_, fss, frs, gss, grs, css, crs, rss, rrs,
):
    az = lax.axis_index("az")
    rad = lax.axis_index("rad")
    mate = rad + 1 - 2 * lax.rem(rad, 2)
    across = lax.rem(rad + 2, NRAD)
    az_up = lax.rem(az + 1, NAZ)
    az_dn = lax.rem(az + NAZ - 1, NAZ)
    rad_up = lax.rem(rad + 1, NRAD)
    rad_dn = lax.rem(rad + NRAD - 1, NRAD)
    axx = lax.rem(az, 4)
    azy = az // 4
    near_peers = [
        ((azy // 2) * 8 + lax.rem(azy + d, 2) * 4 + axx, lax.rem(rad + e, NRAD))
        for d in range(2) for e in range(NRAD) if d or e
    ]
    far_peers = [
        ((lax.rem(azy // 2 + d, 4) * 2 + lax.rem(azy, 2)) * 4 + lax.rem(axx + e, 4), rad)
        for d in range(4) for e in range(4) if d or e
    ]

    def load(f):
        if f < 4:
            src = state.at[f]
        else:
            src = (shear, perm)[f - 4]
        return pltpu.make_async_copy(src, xb.at[f], in_sem.at[f])

    own_basis = pltpu.make_async_copy(basis, own, in_sem.at[7])
    own_basis.start()
    for f in ORDER:
        load(f).start()
    src_load = pltpu.make_async_copy(source, xb.at[6], in_sem.at[6])
    src_load.start()

    barrier = pltpu.get_barrier_semaphore()
    partners = near_peers + far_peers + [(az_up, rad), (az_dn, rad)]
    for peer in partners:
        pl.semaphore_signal(barrier, inc=1, device_id=peer, device_id_type=MESH)
    own_basis.wait()
    values, scale = encode(own[...].reshape(BR // 8, 8, NM))
    code[pl.ds(0, BR), :] = values.reshape(BR, NM)
    code[pl.ds(BR, 16), :] = jnp.concatenate([scale, scale], axis=0)
    pl.semaphore_wait(barrier, len(partners))

    b_across = remote(code, bas.at[rad], bs.at[1], br_.at[1], (az, across))
    b_mate = remote(code, bas.at[rad], bs.at[0], br_.at[0], (az, mate))
    b_relay = remote(bas.at[across], bas.at[across], bs.at[2], br_.at[2], (az, mate))
    b_across.start()
    b_mate.start()

    lane = lax.broadcasted_iota(jnp.int32, (BA, BR), 1)
    zero_row = jnp.zeros((ROW, BR), F32)
    halo = {}
    def stage_field(f):
        load(f).wait()
        ext[f, 0] = zero_row
        ext[f, NH + 1] = zero_row

        def stage(h, q, f=f):
            x = xb[f, h].astype(F32)
            ext[f, h + 1, pl.ds(PAD, BA), :] = x
            ah32[0, pl.ds(h, 1), :] = x[0:1]
            ah32[1, pl.ds(h, 1), :] = x[BA - 1 : BA]
            rolled = pltpu.roll(x, 2 * h + 1, 1)
            return jnp.where(lane // 2 == h, rolled, q)

        q = lax.fori_loop(0, NH, stage, jnp.zeros((BA, BR), F32), unroll=8)
        qs[f] = q.astype(BF16)
        ahs[f, 0] = ah32[0].astype(BF16)
        ahs[f, 1] = ah32[1].astype(BF16)
        one = [
            remote(qs.at[f], ql.at[f], hs.at[f, 0], hr.at[f, 0], (az, rad_up)),
            remote(qs.at[f], qr.at[f], hs.at[f, 1], hr.at[f, 1], (az, rad_dn)),
            remote(ahs.at[f, 1], ahr.at[f, 0], as_.at[f, 0], ar_.at[f, 0], (az_up, rad)),
            remote(ahs.at[f, 0], ahr.at[f, 1], as_.at[f, 1], ar_.at[f, 1], (az_dn, rad)),
        ]
        for c in one:
            c.start()
        halo[f] = one

    for f in ORDER:
        stage_field(f)


    even = lax.rem(lane, 2) == 0

    def finish_halo(f):
        for c in halo[f]:
            c.wait_recv()
        left = jnp.where(rad > 0, ql[f].astype(F32), 0.0)
        right = jnp.where(rad < NRAD - 1, qr[f].astype(F32), 0.0)
        pk[f] = jnp.where(even, pltpu.roll(right, BR - 1, 1), pltpu.roll(left, 1, 1))
        ah32[0] = ahr[f, 0].astype(F32)
        ah32[1] = ahr[f, 1].astype(F32)

        def place(h, carry):
            ext[f, h + 1, pl.ds(PAD - 1, 1), :] = ah32[0, pl.ds(h, 1), :]
            ext[f, h + 1, pl.ds(PAD + BA, 1), :] = ah32[1, pl.ds(h, 1), :]
            return carry

        lax.fori_loop(0, NH, place, 0, unroll=8)

    def split_basis(j, block):
        hi, lo = split(block)
        rows = pl.ds(pl.multiple_of(j * BR, BR), BR)
        bhi[rows, :] = hi
        blo[rows, :] = lo

    def decode_basis(j):
        values = bas[j, pl.ds(0, BR)].astype(F32).reshape(BR // 8, 8, NM)
        scale = bas[j, pl.ds(BR, 16)].astype(F32)[:8]
        split_basis(j, decode(values, scale).reshape(BR, NM))

    split_basis(rad, own[...])
    level = (lax.broadcasted_iota(jnp.int32, (LV, NM), 0) + LV * rad).astype(F32)
    half = jnp.sin(level * (math.pi / (2.0 * NH)))
    sigma = STORAGE + eigen[...] + 4.0 * half * half
    root = jnp.sqrt(sigma * (sigma + 4.0))
    lam = 2.0 / (sigma + 2.0 + root)
    inv_root = 1.0 / root

    lane3 = lax.broadcasted_iota(jnp.int32, (HB, CA, BR), 2)
    first = lane3 == 0
    last = lane3 == BR - 1

    def block(f, h0, c, dh=0, da=0):
        return ext[f, pl.ds(h0 + 1 + dh, HB), pl.ds(PAD + CA * c + da, CA), :]

    def radial_pair(f, h0, c, v):
        tile = pk[f, pl.ds(pl.multiple_of(CA * c, CA), CA), :]
        ends = jnp.stack([pltpu.roll(tile, 127 - 2 * (h0 + i), 1) for i in range(HB)])
        up = jnp.where(last, ends, pltpu.roll(v, BR - 1, 2))
        down = jnp.where(first, ends, pltpu.roll(v, 1, 2))
        return up, down

    def neighbours(f, h0, c):
        v = block(f, h0, c)
        up, down = radial_pair(f, h0, c, v)
        return v, (
            (block(f, h0, c, dh=1), block(f, h0, c, dh=-1)),
            (block(f, h0, c, da=1), block(f, h0, c, da=-1)),
            (up, down),
        )

    src_load.wait()

    def fluid_rows(c, carry):
        def rows(b, carry):
            h0 = b * HB
            k = block(5, h0, c)
            p = block(3, h0, c)
            total = jnp.where(last, 0.0, k + pltpu.roll(k, BR - 1, 2)) * (p - pltpu.roll(p, BR - 1, 2))
            total = total + jnp.where(first, 0.0, k + pltpu.roll(k, 1, 2)) * (p - pltpu.roll(p, 1, 2))
            for move in (dict(dh=1), dict(dh=-1), dict(da=1), dict(da=-1)):
                total = total + (k + block(5, h0, c, **move)) * (p - block(3, h0, c, **move))
            u = block(0, h0, c)
            spread = jnp.where(last, 0.0, pltpu.roll(u, BR - 1, 2)) - jnp.where(first, 0.0, pltpu.roll(u, 1, 2))
            spread = spread + (block(1, h0, c, da=1) - block(1, h0, c, da=-1))
            spread = spread + (block(2, h0, c, dh=1) - block(2, h0, c, dh=-1))
            s = xb[6, pl.ds(h0, HB), pl.ds(pl.multiple_of(CA * c, CA), CA), :].astype(F32)
            res = s + (0.5 * BIOT) * spread + STORAGE * p + 0.5 * total
            tmp[c, pl.ds(pl.multiple_of(h0 * CA, CA), HB * CA), :] = res.reshape(HB * CA, BR)
            return carry

        return lax.fori_loop(0, NH // HB, rows, carry, unroll=8)

    edge = lax.broadcasted_iota(jnp.int32, (CA, BR), 1)
    edge = (edge == 0) | (edge == BR - 1)

    def fluid_send(c, rr):
        tile = cor[pl.ds(pl.multiple_of(CA * c, CA), CA), :]

        def ends(h, rr):
            rows = pl.ds(pl.multiple_of(h * CA, CA), CA)
            res = tmp[c, rows, :] + jnp.where(edge, pltpu.roll(tile, 127 - 2 * h, 1), 0.0)
            tmp[c, rows, :] = res
            return rr + res * res

        rr = lax.fori_loop(0, NH, ends, rr, unroll=8)
        table = fwd_tab[...]
        for pair in range(CA // 2):
            cols = []
            for i in range(2):
                x = tmp[c, pl.ds(2 * pair + i, NH, stride=CA), :]
                hi, lo = split(x)
                cols.append(jnp.concatenate([hi, hi, lo], axis=0))
            y = dot(table, jnp.concatenate(cols, axis=1))
            for i in range(2):
                lev[2 * pair + i] = y[:, BR * i : BR * (i + 1)]
        for d in range(NRAD):
            fs[d, c, pl.ds(0, CA)], fs[d, c, CA] = encode(lev[:, pl.ds(LV * d, LV), :])
        for d in range(1, NRAD):
            fwd_copy(c, d).start()
        return rr

    def fwd_copy(c, d):
        t = lax.rem(rad + d, NRAD)
        return remote(fs.at[t, c], fr.at[rad, c], fss.at[d, c], frs.at[d, c], (az, t))

    lax.fori_loop(1, NCH - 1, fluid_rows, 0)
    for f in ORDER[:4]:
        finish_halo(f)
    beside_k, beside_p, beside_u = pk[5], pk[3], pk[0]
    cor[...] = 0.5 * (qs[5].astype(F32) + beside_k) * (qs[3].astype(F32) - beside_p) + (0.5 * BIOT) * jnp.where(
        even, beside_u, -beside_u
    )
    rr = lax.fori_loop(1, NCH - 1, fluid_send, jnp.zeros((CA, BR), F32))
    b_mate.wait_recv()
    decode_basis(mate)
    b_across.wait_recv()
    b_relay.start()
    decode_basis(across)

    def outer_chunk(n, rr):
        c = n * (NCH - 1)
        fluid_rows(c, 0)
        return fluid_send(c, rr)

    rr = lax.fori_loop(0, 2, outer_chunk, rr)

    for f in ORDER[4:]:
        finish_halo(f)

    def moment_chunk(c, carry):
        def rows(b, carry):
            rr, rz = carry
            h0 = b * HB
            g, gs_ = neighbours(4, h0, c)
            face = [[g + gs_[axis][side] for side in range(2)] for axis in range(3)]
            diag2 = (face[0][0] + face[0][1]) + (face[1][0] + face[1][1]) + (face[2][0] + face[2][1])
            p = block(3, h0, c)
            up, down = radial_pair(3, h0, c, p)
            grads = (
                up - down,
                block(3, h0, c, da=1) - block(3, h0, c, da=-1),
                block(3, h0, c, dh=1) - block(3, h0, c, dh=-1),
            )
            inv = 1.0 / diag2
            square = jnp.zeros_like(p)
            for f in range(3):
                u, us = neighbours(f, h0, c)
                res = -BIOT * grads[f] - diag2 * u
                for axis in range(3):
                    for side in range(2):
                        res = res + face[axis][side] * us[axis][side]
                step = res * inv
                for i in range(HB):
                    out[pl.ds(pl.multiple_of((f * NH + h0 + i) * BA + CA * c, CA), CA), :] = step[i]
                square = square + res * res
            return rr + jnp.sum(square, axis=0), rz + jnp.sum(square * inv, axis=0)

        return lax.fori_loop(0, NH // HB, rows, carry, unroll=8)

    quad = jnp.zeros((CA, BR), F32)
    quad = lax.fori_loop(0, EARLY, moment_chunk, (quad, quad))

    b_relay.wait_recv()
    decode_basis(mate + 2 - 4 * (mate // 2))

    def fwd_chunk(c, carry):
        y, w, power = carry
        for d in range(1, NRAD):
            src = lax.rem(rad + NRAD - d, NRAD)
            remote(fs.at[src, c], fr.at[src, c], fss.at[d, c], frs.at[d, c], (az, src)).wait_recv()
        fr[rad, c] = fs[rad, c]
        for j in range(NRAD):
            scale = fr[j, c, CA]
            for i in range(0, CA, 4):
                x = decode(fr[j, c, pl.ds(i, 4)], scale).reshape(4 * LV, BR)
                hi, lo = split(x)
                xh[pl.ds(i * LV, 4 * LV), pl.ds(j * BR, BR)] = hi
                xl[pl.ds(i * LV, 4 * LV), pl.ds(j * BR, BR)] = lo
        z = dot3(xh[...], xl[...], bhi[...], blo[...], ((1,), (0,)))
        coef[pl.ds(pl.multiple_of(c * CA * LV, CA * LV), CA * LV), :] = z
        for i in range(CA):
            f = z[i * LV : (i + 1) * LV]
            y = lam * y + f
            w = w + power * f
            power = power * lam
        return y, w, power

    zero = jnp.zeros((LV, NM), F32)
    y, w, _ = lax.fori_loop(0, NCH, fwd_chunk, (zero, zero, jnp.ones((LV, NM), F32)))
    cs[0] = y
    cs[1] = w
    c_up = remote(cs.at[0], cr.at[0], css.at[0], crs.at[0], (az_up, rad))
    c_dn = remote(cs.at[1], cr.at[1], css.at[1], crs.at[1], (az_dn, rad))
    c_up.start()
    c_dn.start()
    quad = lax.fori_loop(EARLY, NCH, moment_chunk, quad)
    acc[pl.ds(0, CA), :] = rr + 0.25 * quad[0]
    c_up.wait_recv()

    def sweep_up(a, carry):
        y, yy = carry
        rows = pl.ds(pl.multiple_of(a * LV, LV), LV)
        y = lam * y + coef[rows, :]
        ysol[rows, :] = y
        return y, yy + y * y

    _, yy = lax.fori_loop(0, BA, sweep_up, (cr[0], zero), unroll=8)
    yy = lam * yy
    part = 0.5 * quad[1]
    for j in range(NRAD):
        part = part + yy[:, BR * j : BR * (j + 1)]
    acc[pl.ds(CA, CA), :] = part

    def reduce_copies(slot):
        group, base = ((near_peers, 0), (far_peers, len(near_peers)))[slot]
        return [
            remote(red.at[slot], redr.at[base + i], rss.at[base + i], rrs.at[base + i], peer)
            for i, peer in enumerate(group)
        ], base

    def reduce_finish(slot, total):
        copies, base = reduce_copies(slot)
        for i, c in enumerate(copies):
            c.wait_recv()
            total = total + redr[base + i]
        return total

    red[0] = acc[...]
    for c in reduce_copies(0)[0]:
        c.start()
    c_dn.wait_recv()

    def back_copy(c, d):
        t = lax.rem(rad + d, NRAD)
        return remote(gs.at[t, c], gr.at[rad, c], gss.at[d, c], grs.at[d, c], (az, t))

    def back_chunk(n, w):
        c = NCH - 1 - n

        def cell(i, w):
            a = CA - 1 - i
            rows = pl.ds(pl.multiple_of((c * CA + a) * LV, LV), LV)
            f = coef[rows, :]
            lw = lam * w
            q = (ysol[rows, :] + lw) * inv_root
            gq[pl.ds(pl.multiple_of(a * LV, LV), LV), :] = q
            return f + lw

        w = lax.fori_loop(0, CA, cell, w, unroll=True)
        hi, lo = split(gq[...])
        z = dot3(hi, lo, bhi[...], blo[...], ((1,), (1,)))
        for j in range(NRAD):
            gs[j, c, pl.ds(0, CA)], gs[j, c, CA] = encode(z[:, BR * j : BR * (j + 1)].reshape(CA, LV, BR))
        for d in range(1, NRAD):
            back_copy(c, d).start()
        return w

    lax.fori_loop(0, NCH, back_chunk, cr[1])
    def last_chunk(n, carry):
        c = NCH - 1 - n
        for d in range(1, NRAD):
            src = lax.rem(rad + NRAD - d, NRAD)
            remote(gs.at[src, c], gr.at[src, c], gss.at[d, c], grs.at[d, c], (az, src)).wait_recv()
        gr[rad, c] = gs[rad, c]
        table = inv_tab[...]
        for pair in range(CA // 2):
            cols = []
            for i in range(2):
                a = 2 * pair + i
                x = jnp.concatenate([decode(gr[j, c, a], gr[j, c, CA]) for j in range(NRAD)], axis=0)
                hi, lo = split(x)
                cols.append(jnp.concatenate([hi, hi, lo], axis=0))
            y = dot(table, jnp.concatenate(cols, axis=1))
            for i in range(2):
                out[pl.ds(3 * NH * BA + c * CA + 2 * pair + i, NH, stride=BA), :] = y[:, BR * i : BR * (i + 1)]
        return carry

    total = reduce_finish(0, acc[...])
    red[1] = total
    for c in reduce_copies(1)[0]:
        c.start()
    lax.fori_loop(0, NCH, last_chunk, 0)
    total = reduce_finish(1, total)
    alpha_ref[0, 0] = jnp.sum(total[:CA]) / jnp.sum(total[CA:])

    for one in halo.values():
        for c in one:
            c.wait_send()
    for c in (b_mate, b_across, b_relay, c_up, c_dn):
        c.wait_send()
    for slot in range(2):
        for c in reduce_copies(slot)[0]:
            c.wait_send()

    def drain(c, carry):
        for d in range(1, NRAD):
            fwd_copy(c, d).wait_send()
            back_copy(c, d).wait_send()
        return carry

    lax.fori_loop(0, NCH, drain, 0)


def body(state, source, shear, permeability, radial_basis, radial_eigen):
    fwd_tab, inv_tab = cosine_tables()
    anyspace = pl.BlockSpec(memory_space=pltpu.HBM)
    vmem = pl.BlockSpec(memory_space=pltpu.VMEM)
    dma = pltpu.SemaphoreType.DMA
    scratch = [
        pltpu.VMEM((7, NH, BA, BR), BF16),
        pltpu.VMEM((6, NH + 2, ROW, BR), F32),
        pltpu.VMEM((6, BA, BR), BF16),
        pltpu.VMEM((6, BA, BR), BF16),
        pltpu.VMEM((6, BA, BR), BF16),
        pltpu.VMEM((6, BA, BR), F32),
        pltpu.VMEM((6, 2, NH, BR), BF16),
        pltpu.VMEM((6, 2, NH, BR), BF16),
        pltpu.VMEM((2, NH, BR), F32),
        pltpu.VMEM((NCH, NH * CA, BR), F32),
        pltpu.VMEM((BA, BR), F32),
        pltpu.VMEM((CA, NH, BR), F32),
        pltpu.VMEM((NRAD, NCH, CA + 1, LV, BR), WIRE),
        pltpu.VMEM((NRAD, NCH, CA + 1, LV, BR), WIRE),
        pltpu.VMEM((CA * LV, NM), BF16),
        pltpu.VMEM((CA * LV, NM), BF16),
        pltpu.VMEM((BA * LV, NM), F32),
        pltpu.VMEM((BA * LV, NM), F32),
        pltpu.VMEM((CA * LV, NM), F32),
        pltpu.VMEM((NRAD, NCH, CA + 1, LV, BR), WIRE),
        pltpu.VMEM((NRAD, NCH, CA + 1, LV, BR), WIRE),
        pltpu.VMEM((BR, NM), F32),
        pltpu.VMEM((BR + 16, NM), WIRE),
        pltpu.VMEM((NRAD, BR + 16, NM), WIRE),
        pltpu.VMEM((NM, NM), BF16),
        pltpu.VMEM((NM, NM), BF16),
        pltpu.VMEM((2, LV, NM), F32),
        pltpu.VMEM((2, LV, NM), F32),
        pltpu.VMEM((2 * CA, BR), F32),
        pltpu.VMEM((2, 2 * CA, BR), F32),
        pltpu.VMEM((22, 2 * CA, BR), F32),
        dma((8,)),
        dma((6, 2)), dma((6, 2)), dma((6, 2)), dma((6, 2)),
        dma((3,)), dma((3,)),
        dma((NRAD, NCH)), dma((NRAD, NCH)), dma((NRAD, NCH)), dma((NRAD, NCH)),
        dma((2,)), dma((2,)),
        dma((22,)), dma((22,)),
    ]
    step, alpha = pl.pallas_call(
        kernel,
        out_shape=(pltpu.VMEM((4 * NH * BA, BR), F32), jax.ShapeDtypeStruct((1, 1), F32)),
        in_specs=[anyspace] * 5 + [vmem] * 3,
        out_specs=(vmem, pl.BlockSpec(memory_space=pltpu.SMEM)),
        scratch_shapes=scratch,
        compiler_params=pltpu.CompilerParams(
            collective_id=0, has_side_effects=True, vmem_limit_bytes=52 << 20
        ),
        name="residual_step",
    )(state, source, shear, permeability, radial_basis, radial_eigen.reshape(1, NM), fwd_tab, inv_tab)
    return (alpha[0, 0] * step).astype(BF16).reshape(4, NH, BA, BR)


def solution(mesh):
    placed = (
        P(None, None, "az", "rad"),
        P(None, "az", "rad"),
        P(None, "az", "rad"),
        P(None, "az", "rad"),
        P("rad", None),
        P(),
    )
    return jax.shard_map(
        body, mesh=mesh, in_specs=placed, out_specs=P(None, None, "az", "rad"), check_vma=False
    )
```

```python
import functools
import math

import jax
import jax.numpy as jnp
import numpy as np
from jax import lax
from jax.experimental import pallas as pl
from jax.experimental.pallas import tpu as pltpu
from jax.sharding import PartitionSpec as P

NH = 64
BA = 64
BR = 128
NRAD = 4
NAZ = 32
LV = NH // NRAD
NM = NRAD * BR
CA = 16
NCH = BA // CA
HB = 4
ROW = 80
PAD = 8
EARLY = 2

BIOT = 2.0
STORAGE = 1.0

F32 = jnp.float32
BF16 = jnp.bfloat16
WIRE = BF16
CODE_SPAN = 152.0
CODE_BASE = 68.0
CODE_ZERO = math.exp(-CODE_BASE)
MESH = pl.DeviceIdType.MESH

ORDER = (3, 5, 0, 1, 2, 4)


def split(x):
    hi = x.astype(BF16)
    lo = (x - hi.astype(F32)).astype(BF16)
    return hi, lo


def encode(x):
    size = jnp.abs(x)
    scale = jnp.maximum(jnp.max(size, axis=0), 1e-30).astype(WIRE)
    rate = CODE_SPAN / scale.astype(F32)
    y = jnp.exp(size * rate[None] - CODE_BASE) - CODE_ZERO
    return jnp.where(x < 0, -y, y).astype(WIRE), scale


def decode(y, scale):
    y = y.astype(F32)
    size = jnp.log(jnp.abs(y) + CODE_ZERO) + CODE_BASE
    return jnp.where(y < 0, -size, size) * (scale.astype(F32) * (1.0 / CODE_SPAN))


def cosine_tables():
    l = np.arange(NH, dtype=np.float64)[:, None]
    h = np.arange(NH, dtype=np.float64)[None, :]
    scale = np.where(l == 0, math.sqrt(1.0 / NH), math.sqrt(2.0 / NH))
    table = jnp.asarray(scale * np.cos(math.pi * (h + 0.5) * l / NH), F32)
    out = []
    for c in (table, table.T):
        hi, lo = split(c)
        out.append(jnp.concatenate([hi, lo, hi], axis=1))
    return out


def remote(src, dst, send, recv, device):
    return pltpu.make_async_remote_copy(
        src_ref=src, dst_ref=dst, send_sem=send, recv_sem=recv,
        device_id=device, device_id_type=MESH,
    )


def dot(a, b, dims=((1,), (0,))):
    return lax.dot_general(a, b, (dims, ((), ())), preferred_element_type=F32)


def dot3(xh, xl, bh, bl, dims):
    return dot(xh, bh, dims) + (dot(xl, bh, dims) + dot(xh, bl, dims))


def kernel(
    state, source, shear, perm, basis, eigen, fwd_tab, inv_tab, out, alpha_ref,
    xb, ext, qs, ql, qr, pk, ahs, ahr, ah32,
    tmp, cor, lev, fs, fr, xh, xl, coef, ysol, gq, gs, gr,
    own, code, bas, bhi, blo, cs, cr, acc, red, redr,
    in_sem, hs, hr, as_, ar_, bs, br_, fss, frs, gss, grs, css, crs, rss, rrs,
):
    az = lax.axis_index("az")
    rad = lax.axis_index("rad")
    mate = rad + 1 - 2 * lax.rem(rad, 2)
    across = lax.rem(rad + 2, NRAD)
    az_up = lax.rem(az + 1, NAZ)
    az_dn = lax.rem(az + NAZ - 1, NAZ)
    rad_up = lax.rem(rad + 1, NRAD)
    rad_dn = lax.rem(rad + NRAD - 1, NRAD)
    axx = lax.rem(az, 4)
    azy = az // 4
    near_peers = [
        ((azy // 2) * 8 + lax.rem(azy + d, 2) * 4 + axx, lax.rem(rad + e, NRAD))
        for d in range(2) for e in range(NRAD) if d or e
    ]
    far_peers = [
        ((lax.rem(azy // 2 + d, 4) * 2 + lax.rem(azy, 2)) * 4 + lax.rem(axx + e, 4), rad)
        for d in range(4) for e in range(4) if d or e
    ]

    def load(f):
        if f < 4:
            src = state.at[f]
        else:
            src = (shear, perm)[f - 4]
        return pltpu.make_async_copy(src, xb.at[f], in_sem.at[f])

    own_basis = pltpu.make_async_copy(basis, own, in_sem.at[7])
    own_basis.start()
    for f in ORDER:
        load(f).start()
    src_load = pltpu.make_async_copy(source, xb.at[6], in_sem.at[6])
    src_load.start()

    barrier = pltpu.get_barrier_semaphore()
    partners = near_peers + far_peers + [(az_up, rad), (az_dn, rad)]
    for peer in partners:
        pl.semaphore_signal(barrier, inc=1, device_id=peer, device_id_type=MESH)
    own_basis.wait()
    values, scale = encode(own[...].reshape(BR // 8, 8, NM))
    code[pl.ds(0, BR), :] = values.reshape(BR, NM)
    code[pl.ds(BR, 16), :] = jnp.concatenate([scale, scale], axis=0)
    pl.semaphore_wait(barrier, len(partners))

    b_across = remote(code, bas.at[rad], bs.at[1], br_.at[1], (az, across))
    b_mate = remote(code, bas.at[rad], bs.at[0], br_.at[0], (az, mate))
    b_relay = remote(bas.at[across], bas.at[across], bs.at[2], br_.at[2], (az, mate))
    b_across.start()
    b_mate.start()

    lane = lax.broadcasted_iota(jnp.int32, (BA, BR), 1)
    zero_row = jnp.zeros((ROW, BR), F32)
    halo = {}
    def stage_field(f):
        load(f).wait()
        ext[f, 0] = zero_row
        ext[f, NH + 1] = zero_row

        def stage(h, q, f=f):
            x = xb[f, h].astype(F32)
            ext[f, h + 1, pl.ds(PAD, BA), :] = x
            ah32[0, pl.ds(h, 1), :] = x[0:1]
            ah32[1, pl.ds(h, 1), :] = x[BA - 1 : BA]
            rolled = pltpu.roll(x, 2 * h + 1, 1)
            return jnp.where(lane // 2 == h, rolled, q)

        q = lax.fori_loop(0, NH, stage, jnp.zeros((BA, BR), F32), unroll=8)
        qs[f] = q.astype(BF16)
        ahs[f, 0] = ah32[0].astype(BF16)
        ahs[f, 1] = ah32[1].astype(BF16)
        one = [
            remote(qs.at[f], ql.at[f], hs.at[f, 0], hr.at[f, 0], (az, rad_up)),
            remote(qs.at[f], qr.at[f], hs.at[f, 1], hr.at[f, 1], (az, rad_dn)),
            remote(ahs.at[f, 1], ahr.at[f, 0], as_.at[f, 0], ar_.at[f, 0], (az_up, rad)),
            remote(ahs.at[f, 0], ahr.at[f, 1], as_.at[f, 1], ar_.at[f, 1], (az_dn, rad)),
        ]
        for c in one:
            c.start()
        halo[f] = one

    for f in ORDER:
        stage_field(f)


    even = lax.rem(lane, 2) == 0

    def finish_columns(f):
        for c in halo[f][:2]:
            c.wait_recv()
        left = jnp.where(rad > 0, ql[f].astype(F32), 0.0)
        right = jnp.where(rad < NRAD - 1, qr[f].astype(F32), 0.0)
        pk[f] = jnp.where(even, pltpu.roll(right, BR - 1, 1), pltpu.roll(left, 1, 1))

    def finish_rows(f):
        for c in halo[f][2:]:
            c.wait_recv()
        ah32[0] = ahr[f, 0].astype(F32)
        ah32[1] = ahr[f, 1].astype(F32)

        def place(h, carry):
            ext[f, h + 1, pl.ds(PAD - 1, 1), :] = ah32[0, pl.ds(h, 1), :]
            ext[f, h + 1, pl.ds(PAD + BA, 1), :] = ah32[1, pl.ds(h, 1), :]
            return carry

        lax.fori_loop(0, NH, place, 0, unroll=8)

    def split_basis(j, block):
        hi, lo = split(block)
        rows = pl.ds(pl.multiple_of(j * BR, BR), BR)
        bhi[rows, :] = hi
        blo[rows, :] = lo

    def decode_basis(j):
        values = bas[j, pl.ds(0, BR)].astype(F32).reshape(BR // 8, 8, NM)
        scale = bas[j, pl.ds(BR, 16)].astype(F32)[:8]
        split_basis(j, decode(values, scale).reshape(BR, NM))

    split_basis(rad, own[...])
    level = (lax.broadcasted_iota(jnp.int32, (LV, NM), 0) + LV * rad).astype(F32)
    half = jnp.sin(level * (math.pi / (2.0 * NH)))
    sigma = STORAGE + eigen[...] + 4.0 * half * half
    root = jnp.sqrt(sigma * (sigma + 4.0))
    lam = 2.0 / (sigma + 2.0 + root)
    inv_root = 1.0 / root

    lane3 = lax.broadcasted_iota(jnp.int32, (HB, CA, BR), 2)
    first = lane3 == 0
    last = lane3 == BR - 1

    def block(f, h0, c, dh=0, da=0):
        return ext[f, pl.ds(h0 + 1 + dh, HB), pl.ds(PAD + CA * c + da, CA), :]

    def column(f, h0, c):
        planes = ext[f, pl.ds(h0, HB + 2), pl.ds(pl.multiple_of(PAD + CA * c, PAD), CA), :]
        return planes[:HB], planes[1 : HB + 1], planes[2:]

    def radial_pair(f, h0, c, v):
        tile = pk[f, pl.ds(pl.multiple_of(CA * c, CA), CA), :]
        ends = jnp.stack([pltpu.roll(tile, 127 - 2 * (h0 + i), 1) for i in range(HB)])
        up = jnp.where(last, ends, pltpu.roll(v, BR - 1, 2))
        down = jnp.where(first, ends, pltpu.roll(v, 1, 2))
        return up, down

    def neighbours(f, h0, c):
        below, v, above = column(f, h0, c)
        up, down = radial_pair(f, h0, c, v)
        return v, (
            (above, below),
            (block(f, h0, c, da=1), block(f, h0, c, da=-1)),
            (up, down),
        )

    src_load.wait()

    def fluid_rows(c, carry):
        def rows(b, carry):
            h0 = b * HB
            k_below, k, k_above = column(5, h0, c)
            p_below, p, p_above = column(3, h0, c)
            total = jnp.where(last, 0.0, k + pltpu.roll(k, BR - 1, 2)) * (p - pltpu.roll(p, BR - 1, 2))
            total = total + jnp.where(first, 0.0, k + pltpu.roll(k, 1, 2)) * (p - pltpu.roll(p, 1, 2))
            total = total + (k + k_above) * (p - p_above)
            total = total + (k + k_below) * (p - p_below)
            for da in (1, -1):
                total = total + (k + block(5, h0, c, da=da)) * (p - block(3, h0, c, da=da))
            u = block(0, h0, c)
            spread = jnp.where(last, 0.0, pltpu.roll(u, BR - 1, 2)) - jnp.where(first, 0.0, pltpu.roll(u, 1, 2))
            spread = spread + (block(1, h0, c, da=1) - block(1, h0, c, da=-1))
            spread = spread + (block(2, h0, c, dh=1) - block(2, h0, c, dh=-1))
            s = xb[6, pl.ds(h0, HB), pl.ds(pl.multiple_of(CA * c, CA), CA), :].astype(F32)
            res = s + (0.5 * BIOT) * spread + STORAGE * p + 0.5 * total
            tmp[c, pl.ds(pl.multiple_of(h0 * CA, CA), HB * CA), :] = res.reshape(HB * CA, BR)
            return carry

        return lax.fori_loop(0, NH // HB, rows, carry, unroll=8)

    edge = lax.broadcasted_iota(jnp.int32, (CA, BR), 1)
    edge = (edge == 0) | (edge == BR - 1)

    def fluid_send(c, rr):
        tile = cor[pl.ds(pl.multiple_of(CA * c, CA), CA), :]

        def ends(h, rr):
            rows = pl.ds(pl.multiple_of(h * CA, CA), CA)
            res = tmp[c, rows, :] + jnp.where(edge, pltpu.roll(tile, 127 - 2 * h, 1), 0.0)
            tmp[c, rows, :] = res
            return rr + res * res

        rr = lax.fori_loop(0, NH, ends, rr, unroll=8)
        table = fwd_tab[...]
        for pair in range(CA // 2):
            cols = []
            for i in range(2):
                x = tmp[c, pl.ds(2 * pair + i, NH, stride=CA), :]
                hi, lo = split(x)
                cols.append(jnp.concatenate([hi, hi, lo], axis=0))
            y = dot(table, jnp.concatenate(cols, axis=1))
            for i in range(2):
                lev[2 * pair + i] = y[:, BR * i : BR * (i + 1)]
        for d in range(NRAD):
            fs[d, c, pl.ds(0, CA)], fs[d, c, CA] = encode(lev[:, pl.ds(LV * d, LV), :])
        for d in range(1, NRAD):
            fwd_copy(c, d).start()
        return rr

    def fwd_copy(c, d):
        t = lax.rem(rad + d, NRAD)
        return remote(fs.at[t, c], fr.at[rad, c], fss.at[d, c], frs.at[d, c], (az, t))

    lax.fori_loop(1, NCH - 1, fluid_rows, 0)
    for f in ORDER[:3]:
        finish_columns(f)
    beside_k, beside_p, beside_u = pk[5], pk[3], pk[0]
    cor[...] = 0.5 * (qs[5].astype(F32) + beside_k) * (qs[3].astype(F32) - beside_p) + (0.5 * BIOT) * jnp.where(
        even, beside_u, -beside_u
    )
    rr = lax.fori_loop(1, NCH - 1, fluid_send, jnp.zeros((CA, BR), F32))
    for f in (3, 5, 1):
        finish_rows(f)
    b_mate.wait_recv()
    decode_basis(mate)
    b_across.wait_recv()
    b_relay.start()
    decode_basis(across)

    def outer_chunk(n, rr):
        c = n * (NCH - 1)
        fluid_rows(c, 0)
        return fluid_send(c, rr)

    rr = lax.fori_loop(0, 2, outer_chunk, rr)

    for f in (1, 2, 4):
        finish_columns(f)
    for f in (0, 2, 4):
        finish_rows(f)

    def moment_chunk(c, carry):
        def rows(b, carry):
            rr, rz = carry
            h0 = b * HB
            g, gs_ = neighbours(4, h0, c)
            face = [[g + gs_[axis][side] for side in range(2)] for axis in range(3)]
            diag2 = (face[0][0] + face[0][1]) + (face[1][0] + face[1][1]) + (face[2][0] + face[2][1])
            p_below, p, p_above = column(3, h0, c)
            up, down = radial_pair(3, h0, c, p)
            grads = (
                up - down,
                block(3, h0, c, da=1) - block(3, h0, c, da=-1),
                p_above - p_below,
            )
            inv = 1.0 / diag2
            square = jnp.zeros_like(p)
            for f in range(3):
                u, us = neighbours(f, h0, c)
                res = -BIOT * grads[f] - diag2 * u
                for axis in range(3):
                    for side in range(2):
                        res = res + face[axis][side] * us[axis][side]
                step = res * inv
                for i in range(HB):
                    out[pl.ds(pl.multiple_of((f * NH + h0 + i) * BA + CA * c, CA), CA), :] = step[i]
                square = square + res * res
            return rr + jnp.sum(square, axis=0), rz + jnp.sum(square * inv, axis=0)

        return lax.fori_loop(0, NH // HB, rows, carry, unroll=8)

    quad = jnp.zeros((CA, BR), F32)
    quad = lax.fori_loop(0, EARLY, moment_chunk, (quad, quad))

    b_relay.wait_recv()
    decode_basis(mate + 2 - 4 * (mate // 2))

    def fwd_chunk(c, carry):
        y, w, power = carry
        for d in range(1, NRAD):
            src = lax.rem(rad + NRAD - d, NRAD)
            remote(fs.at[src, c], fr.at[src, c], fss.at[d, c], frs.at[d, c], (az, src)).wait_recv()
        fr[rad, c] = fs[rad, c]
        for j in range(NRAD):
            scale = fr[j, c, CA]
            for i in range(0, CA, 4):
                x = decode(fr[j, c, pl.ds(i, 4)], scale).reshape(4 * LV, BR)
                hi, lo = split(x)
                xh[pl.ds(i * LV, 4 * LV), pl.ds(j * BR, BR)] = hi
                xl[pl.ds(i * LV, 4 * LV), pl.ds(j * BR, BR)] = lo
        z = dot3(xh[...], xl[...], bhi[...], blo[...], ((1,), (0,)))
        coef[pl.ds(pl.multiple_of(c * CA * LV, CA * LV), CA * LV), :] = z
        for i in range(CA):
            f = z[i * LV : (i + 1) * LV]
            y = lam * y + f
            w = w + power * f
            power = power * lam
        return y, w, power

    zero = jnp.zeros((LV, NM), F32)
    y, w, _ = lax.fori_loop(0, NCH, fwd_chunk, (zero, zero, jnp.ones((LV, NM), F32)))
    cs[0] = y
    cs[1] = w
    c_up = remote(cs.at[0], cr.at[0], css.at[0], crs.at[0], (az_up, rad))
    c_dn = remote(cs.at[1], cr.at[1], css.at[1], crs.at[1], (az_dn, rad))
    c_up.start()
    c_dn.start()
    quad = lax.fori_loop(EARLY, NCH, moment_chunk, quad)
    acc[pl.ds(0, CA), :] = rr + 0.25 * quad[0]
    c_up.wait_recv()

    def sweep_up(a, carry):
        y, yy = carry
        rows = pl.ds(pl.multiple_of(a * LV, LV), LV)
        y = lam * y + coef[rows, :]
        ysol[rows, :] = y
        return y, yy + y * y

    _, yy = lax.fori_loop(0, BA, sweep_up, (cr[0], zero), unroll=8)
    yy = lam * yy
    part = 0.5 * quad[1]
    for j in range(NRAD):
        part = part + yy[:, BR * j : BR * (j + 1)]
    acc[pl.ds(CA, CA), :] = part

    def reduce_copies(slot):
        group, base = ((near_peers, 0), (far_peers, len(near_peers)))[slot]
        return [
            remote(red.at[slot], redr.at[base + i], rss.at[base + i], rrs.at[base + i], peer)
            for i, peer in enumerate(group)
        ], base

    def reduce_finish(slot, total):
        copies, base = reduce_copies(slot)
        for i, c in enumerate(copies):
            c.wait_recv()
            total = total + redr[base + i]
        return total

    red[0] = acc[...]
    for c in reduce_copies(0)[0]:
        c.start()
    c_dn.wait_recv()

    def back_copy(c, d):
        t = lax.rem(rad + d, NRAD)
        return remote(gs.at[t, c], gr.at[rad, c], gss.at[d, c], grs.at[d, c], (az, t))

    def back_chunk(n, w):
        c = NCH - 1 - n

        def cell(i, w):
            a = CA - 1 - i
            rows = pl.ds(pl.multiple_of((c * CA + a) * LV, LV), LV)
            f = coef[rows, :]
            lw = lam * w
            q = (ysol[rows, :] + lw) * inv_root
            gq[pl.ds(pl.multiple_of(a * LV, LV), LV), :] = q
            return f + lw

        w = lax.fori_loop(0, CA, cell, w, unroll=True)
        hi, lo = split(gq[...])
        z = dot3(hi, lo, bhi[...], blo[...], ((1,), (1,)))
        for j in range(NRAD):
            gs[j, c, pl.ds(0, CA)], gs[j, c, CA] = encode(z[:, BR * j : BR * (j + 1)].reshape(CA, LV, BR))
        for d in range(1, NRAD):
            back_copy(c, d).start()
        return w

    lax.fori_loop(0, NCH, back_chunk, cr[1])
    def last_chunk(n, carry):
        c = NCH - 1 - n
        for d in range(1, NRAD):
            src = lax.rem(rad + NRAD - d, NRAD)
            remote(gs.at[src, c], gr.at[src, c], gss.at[d, c], grs.at[d, c], (az, src)).wait_recv()
        gr[rad, c] = gs[rad, c]
        table = inv_tab[...]
        for pair in range(CA // 2):
            cols = []
            for i in range(2):
                a = 2 * pair + i
                x = jnp.concatenate([decode(gr[j, c, a], gr[j, c, CA]) for j in range(NRAD)], axis=0)
                hi, lo = split(x)
                cols.append(jnp.concatenate([hi, hi, lo], axis=0))
            y = dot(table, jnp.concatenate(cols, axis=1))
            for i in range(2):
                out[pl.ds(3 * NH * BA + c * CA + 2 * pair + i, NH, stride=BA), :] = y[:, BR * i : BR * (i + 1)]
        return carry

    total = reduce_finish(0, acc[...])
    red[1] = total
    for c in reduce_copies(1)[0]:
        c.start()
    lax.fori_loop(0, NCH, last_chunk, 0)
    total = reduce_finish(1, total)
    alpha_ref[0, 0] = jnp.sum(total[:CA]) / jnp.sum(total[CA:])

    for one in halo.values():
        for c in one:
            c.wait_send()
    for c in (b_mate, b_across, b_relay, c_up, c_dn):
        c.wait_send()
    for slot in range(2):
        for c in reduce_copies(slot)[0]:
            c.wait_send()

    def drain(c, carry):
        for d in range(1, NRAD):
            fwd_copy(c, d).wait_send()
            back_copy(c, d).wait_send()
        return carry

    lax.fori_loop(0, NCH, drain, 0)


def body(state, source, shear, permeability, radial_basis, radial_eigen):
    fwd_tab, inv_tab = cosine_tables()
    anyspace = pl.BlockSpec(memory_space=pltpu.HBM)
    vmem = pl.BlockSpec(memory_space=pltpu.VMEM)
    dma = pltpu.SemaphoreType.DMA
    scratch = [
        pltpu.VMEM((7, NH, BA, BR), BF16),
        pltpu.VMEM((6, NH + 2, ROW, BR), F32),
        pltpu.VMEM((6, BA, BR), BF16),
        pltpu.VMEM((6, BA, BR), BF16),
        pltpu.VMEM((6, BA, BR), BF16),
        pltpu.VMEM((6, BA, BR), F32),
        pltpu.VMEM((6, 2, NH, BR), BF16),
        pltpu.VMEM((6, 2, NH, BR), BF16),
        pltpu.VMEM((2, NH, BR), F32),
        pltpu.VMEM((NCH, NH * CA, BR), F32),
        pltpu.VMEM((BA, BR), F32),
        pltpu.VMEM((CA, NH, BR), F32),
        pltpu.VMEM((NRAD, NCH, CA + 1, LV, BR), WIRE),
        pltpu.VMEM((NRAD, NCH, CA + 1, LV, BR), WIRE),
        pltpu.VMEM((CA * LV, NM), BF16),
        pltpu.VMEM((CA * LV, NM), BF16),
        pltpu.VMEM((BA * LV, NM), F32),
        pltpu.VMEM((BA * LV, NM), F32),
        pltpu.VMEM((CA * LV, NM), F32),
        pltpu.VMEM((NRAD, NCH, CA + 1, LV, BR), WIRE),
        pltpu.VMEM((NRAD, NCH, CA + 1, LV, BR), WIRE),
        pltpu.VMEM((BR, NM), F32),
        pltpu.VMEM((BR + 16, NM), WIRE),
        pltpu.VMEM((NRAD, BR + 16, NM), WIRE),
        pltpu.VMEM((NM, NM), BF16),
        pltpu.VMEM((NM, NM), BF16),
        pltpu.VMEM((2, LV, NM), F32),
        pltpu.VMEM((2, LV, NM), F32),
        pltpu.VMEM((2 * CA, BR), F32),
        pltpu.VMEM((2, 2 * CA, BR), F32),
        pltpu.VMEM((22, 2 * CA, BR), F32),
        dma((8,)),
        dma((6, 2)), dma((6, 2)), dma((6, 2)), dma((6, 2)),
        dma((3,)), dma((3,)),
        dma((NRAD, NCH)), dma((NRAD, NCH)), dma((NRAD, NCH)), dma((NRAD, NCH)),
        dma((2,)), dma((2,)),
        dma((22,)), dma((22,)),
    ]
    step, alpha = pl.pallas_call(
        kernel,
        out_shape=(pltpu.VMEM((4 * NH * BA, BR), F32), jax.ShapeDtypeStruct((1, 1), F32)),
        in_specs=[anyspace] * 5 + [vmem] * 3,
        out_specs=(vmem, pl.BlockSpec(memory_space=pltpu.SMEM)),
        scratch_shapes=scratch,
        compiler_params=pltpu.CompilerParams(
            collective_id=0, has_side_effects=True, vmem_limit_bytes=52 << 20
        ),
        name="residual_step",
    )(state, source, shear, permeability, radial_basis, radial_eigen.reshape(1, NM), fwd_tab, inv_tab)
    return (alpha[0, 0] * step).astype(BF16).reshape(4, NH, BA, BR)


def solution(mesh):
    placed = (
        P(None, None, "az", "rad"),
        P(None, "az", "rad"),
        P(None, "az", "rad"),
        P(None, "az", "rad"),
        P("rad", None),
        P(),
    )
    return jax.shard_map(
        body, mesh=mesh, in_specs=placed, out_specs=P(None, None, "az", "rad"), check_vma=False
    )
```
